32 devices in a mesh: dp: 8 (over y, x, core), tp: 4 (over z).
Axes of the slice: x: 2, y: 2, z: 4, core: 2. Of those that a mesh axis runs over, the one named last changes fastest.
Arguments:
- hidden_in: bfloat16 [24, 512, 768], P('dp', 'tp'), may hold values from -6 to 6
- lengths: int32 [24], P('dp'), may hold values from 256 to 512, as said below
- inst_lengths: int32 [24], P('dp'), may hold values from 5 to 40
- w_query: bfloat16 [768, 768], P(None, 'tp'), may hold values from -0.0546875 to 0.0546875
- w_key: bfloat16 [768, 768], P(None, 'tp'), may hold values from -0.15625 to 0.15625
- w_value: bfloat16 [768, 768], P(None, 'tp'), may hold values from -0.21875 to 0.21875
- attention_output_weight: bfloat16 [768, 768], P('tp'), may hold values from -0.75 to 0.75
- feedforward_input_weight: bfloat16 [768, 3072], P(None, 'tp'), may hold values from -0.21875 to 0.21875
- feedforward_output_weight: bfloat16 [3072, 768], P('tp'), may hold values from -0.109375 to 0.109375
- rel_table: bfloat16 [32, 12], P(None, 'tp'), may hold values from -4 to 4
- gain_attn: bfloat16 [768], replicated, may hold values from 0.5 to 1.5
- gain_ffn: bfloat16 [768], replicated, may hold values from 0.5 to 1.5
- grad_output: bfloat16 [24, 512, 768], P('dp', 'tp'), may hold values from -6 to 6
- grad_pooled: bfloat16 [24, 768], P('dp', 'tp'), may hold values from -192 to 192
Outputs:
- layer_out: bfloat16 [24, 512, 768], P('dp', 'tp')
- pooled: float32 [24, 768], P('dp', 'tp')
- grad_hidden: float32 [24, 512, 768], P('dp', 'tp')
- grad_w_query: float32 [768, 768], P(None, 'tp')
- grad_w_key: float32 [768, 768], P(None, 'tp')
- grad_w_value: float32 [768, 768], P(None, 'tp')
- grad_w_out: float32 [768, 768], P('tp')
- grad_w_in: float32 [768, 3072], P(None, 'tp')
- grad_w_ffn_out: float32 [3072, 768], P('tp')
- grad_table: float32 [32, 12], P(None, 'tp')
- grad_gain_attn: float32 [768], replicated
- grad_gain_ffn: float32 [768], replicated
The draws below stay inside these ranges and needn't reach their ends.
Inputs may be any that keep to these rules, and one draw needn't show every extreme that they name: `lengths`: some row in every draw has length 512.
All inputs are finite; a program needn't handle non-finite values.
Results may differ from the reference program's by a relative error of at most 0.019.
Values may be sent and summed in bfloat16 or wider, within the bound.
No kernel may reach another device: no remote copies, remote signals or barrier semaphores. Data moves between devices by JAX's collectives and lax.ppermute only.
A program may use at most 128 MiB of HBM per device.

```python
import jax
import jax.numpy as jnp
from jax import lax

D = 768
NH = 12
HD = 64
FF = 3072
NB = 32
LEN = 512
ROWS = 24


def draw_lengths(key, part):
    spread = jax.random.randint(key, (ROWS,), LEN // 2, LEN + 1, dtype=jnp.int32)
    chosen = jax.random.randint(jax.random.fold_in(key, 7), (), 0, ROWS, dtype=jnp.int32)
    return jnp.where(jnp.arange(ROWS, dtype=jnp.int32) == chosen, LEN, spread).astype(jnp.int32)


def set_ends(values, stream_key, least, high):
    longest = values.shape.index(max(values.shape))
    spots = []
    for shift in (0, 1):
        where = [jax.random.randint(jax.random.fold_in(stream_key, axis), (), 0, length) for axis, length in enumerate(values.shape)]
        where[longest] = (where[longest] + shift) % values.shape[longest]
        spots.append(tuple(where))
    return values.at[spots[0]].set(least).at[spots[1]].set(high)


def block_levels(stream_key, shape, shards, smallest, largest):
    level, own = 1.0, jax.random.fold_in(stream_key, 6)
    for axis_at, blocks in shards:
        heights = jnp.exp(jax.random.uniform(jax.random.fold_in(own, axis_at), (blocks,), jnp.float32, smallest / len(shards), largest / len(shards)))
        level = level * jnp.repeat(heights, shape[axis_at] // blocks).reshape([-1 if axis == axis_at else 1 for axis in range(len(shape))])
    return level


def gaussian(stream_key, shape, scale, limit, cuts=(), kind=jnp.bfloat16):
    level = block_levels(stream_key, shape, cuts, -0.22, 0.18) if cuts else 1.0
    entries = jax.random.normal(stream_key, shape, jnp.float32) * scale * level
    return jnp.minimum(jnp.maximum(entries, -limit), limit).astype(kind)


def setup_inputs(seed: int = 0) -> dict:
    seeds = jax.random.split(jax.random.key(seed), 15)
    return {
        "hidden_in": gaussian(seeds[0], (ROWS, LEN, D), 1.0, 6.0, ((0, 8), (1, 4))),
        "lengths": draw_lengths(jax.random.fold_in(seeds[14], 71), 0),
        "inst_lengths": set_ends(jax.random.randint(seeds[2], (ROWS,), 5, 41), jax.random.fold_in(seeds[2], 1), 5, 40).astype(jnp.int32),
        "w_query": gaussian(seeds[3], (D, NH * HD), (16 * D) ** -0.5, 0.0546875, ((1, 4),)),
        "w_key": gaussian(seeds[4], (D, NH * HD), (2 * D) ** -0.5, 0.15625, ((1, 4),)),
        "w_value": gaussian(seeds[5], (D, NH * HD), D ** -0.5, 0.21875, ((1, 4),)),
        "attention_output_weight": gaussian(seeds[6], (NH * HD, D), HD ** -0.5, 0.75, ((0, 4),)),
        "feedforward_input_weight": gaussian(seeds[7], (D, FF), D ** -0.5, 0.21875, ((1, 4),)),
        "feedforward_output_weight": gaussian(seeds[8], (FF, D), FF ** -0.5, 0.109375, ((0, 4),)),
        "rel_table": gaussian(seeds[9], (NB, NH), 1.0, 4.0, ((1, 4),)),
        "gain_attn": jnp.clip(1.0 + 0.1 * jax.random.normal(seeds[10], (D,), jnp.float32), 0.5, 1.5).astype(jnp.bfloat16),
        "gain_ffn": jnp.clip(1.0 + 0.1 * jax.random.normal(seeds[11], (D,), jnp.float32), 0.5, 1.5).astype(jnp.bfloat16),
        "grad_output": gaussian(seeds[12], (ROWS, LEN, D), 1.0, 6.0, ((0, 8), (1, 4))),
        "grad_pooled": gaussian(seeds[13], (ROWS, D), (LEN // 16), 192.0, ((0, 8), (1, 4))),
    }


@jax.custom_vjp
def low(v):
    return lax.optimization_barrier(v.astype(jnp.bfloat16)).astype(jnp.float32)

@jax.custom_vjp
def low_back(v):
    return v

def low_keep(v):
    return (low(v), None)

def low_pass(kept, grad):
    return (grad,)

def back_keep(v):
    return (v, None)

def back_low(kept, grad):
    return (low(grad),)
low.defvjp(low_keep, low_pass)
low_back.defvjp(back_keep, back_low)

def bucket_codes(size):
    places = jnp.arange(size, dtype=jnp.int32)
    offset = places[None, :] - places[:, None]
    upper_half = jnp.where(offset > 0, 16, 0).astype(jnp.int32)
    distance = jnp.abs(offset)
    far_code = 8 + sum(((distance >= threshold).astype(jnp.int32) for threshold in (12, 16, 23, 32, 46, 64, 91)))
    return upper_half + jnp.where(distance < 8, distance, far_code)

def rms_scale(values, gain):
    return values * lax.rsqrt(lax.optimization_barrier(jnp.mean(values * values, axis=-1, keepdims=True)) + 1e-06) * gain

def gelu_of(values):
    return jax.nn.gelu(values, approximate=True)

def block_forward(hidden, row_lengths, row_insts, w_query, w_key, w_value, attention_output_weight, feedforward_input_weight, feedforward_output_weight, rel_table, gain_attn, gain_ffn):
    top_precision = lax.Precision.HIGHEST
    seq_count, full_len, model_width = hidden.shape
    head_count = rel_table.shape[1]
    head_size = w_query.shape[1] // head_count
    first_normalized = low(rms_scale(hidden, gain_attn))

    def project(weight_matrix):
        combined_projection = jnp.einsum('vrf,fp->vrp', first_normalized, weight_matrix, precision=top_precision)
        return low_back(low(combined_projection)).reshape(seq_count, full_len, head_count, head_size)
    queries = project(w_query)
    key_heads = project(w_key)
    value_heads = project(w_value)
    codes = bucket_codes(full_len)
    bias = jnp.transpose(rel_table[codes], (2, 0, 1))
    places = jnp.arange(full_len, dtype=jnp.int32)
    key_valid = places[None, :] < row_lengths[:, None]

    def attend(pieces):
        query_one, key_one, value_one, valid_one = pieces
        scores = low_back(jnp.einsum('qhe,khe->hqk', query_one, key_one, precision=top_precision) + bias)
        scores = jnp.where(valid_one[None, None, :], scores, -1000000000.0)
        row_max = lax.optimization_barrier(jnp.max(scores, axis=-1, keepdims=True))
        exp_scores = jnp.exp(scores - row_max)
        attn_probs = exp_scores / lax.optimization_barrier(jnp.sum(exp_scores, axis=-1, keepdims=True))
        return jnp.einsum('hqk,khe->qhe', low(attn_probs), value_one, precision=top_precision)
    attention_mixture = lax.map(jax.checkpoint(attend), (queries, key_heads, value_heads, key_valid))
    attention_mixture = low_back(low(attention_mixture.reshape(seq_count, full_len, head_count * head_size)))
    residual_branch = low_back(jnp.einsum('wcr,rg->wcg', attention_mixture, attention_output_weight, precision=top_precision))
    middle = hidden + residual_branch
    second_normalized = low(rms_scale(middle, gain_ffn))
    feedforward_activation = low_back(jnp.einsum('wgu,uz->wgz', second_normalized, feedforward_input_weight, precision=top_precision))
    gelu_output = low_back(low(gelu_of(feedforward_activation)))
    feedforward_branch = low_back(jnp.einsum('jpi,ic->jpc', gelu_output, feedforward_output_weight, precision=top_precision))
    result = middle + feedforward_branch
    pool_mask = ((places[None, :] >= row_insts[:, None]) & key_valid).astype(jnp.float32)
    counts = (row_lengths - row_insts).astype(jnp.float32)
    pooled = lax.optimization_barrier(jnp.sum(result * pool_mask[:, :, None], axis=1)) / counts[:, None]
    return (result, pooled)

def reference(hidden_in, lengths, inst_lengths, w_query, w_key, w_value, attention_output_weight, feedforward_input_weight, feedforward_output_weight, rel_table, gain_attn, gain_ffn, grad_output, grad_pooled):
    weights = tuple((weight_matrix.astype(jnp.float32) for weight_matrix in (w_query, w_key, w_value, attention_output_weight, feedforward_input_weight, feedforward_output_weight, rel_table, gain_attn, gain_ffn)))
    group_size = 8
    blocks = hidden_in.shape[0] // group_size

    def by_group(values):
        return values.reshape((blocks, group_size) + values.shape[1:])

    def one_group(totals, pieces):
        hidden, row_lengths, row_insts, cot_rows, cot_pool = pieces

        def forward(hidden_f, *params):
            return block_forward(hidden_f, row_lengths, row_insts, *params)
        (result, pooled), pullback = jax.vjp(forward, hidden.astype(jnp.float32), *weights)
        gradients = pullback((cot_rows.astype(jnp.float32), cot_pool.astype(jnp.float32)))
        totals = tuple((left + right for left, right in zip(totals, gradients[1:])))
        return (totals, (result.astype(jnp.bfloat16), pooled, gradients[0]))
    zero_totals = tuple((jnp.zeros(weight_matrix.shape, jnp.float32) for weight_matrix in weights))
    totals, (layer_rows, pooled_rows, grad_rows) = lax.scan(one_group, zero_totals, (by_group(hidden_in), by_group(lengths), by_group(inst_lengths), by_group(grad_output), by_group(grad_pooled)))
    return (layer_rows.reshape(hidden_in.shape), pooled_rows.reshape(grad_pooled.shape), grad_rows.reshape(hidden_in.shape), totals[0], totals[1], totals[2], totals[3], totals[4], totals[5], totals[6], totals[7], totals[8])
```

```python
import functools

import jax
import jax.numpy as jnp
from jax import lax
from jax.experimental import pallas as pl
from jax.experimental.pallas import tpu as pltpu
from jax.sharding import PartitionSpec as P

F32 = jnp.float32
BF16 = jnp.bfloat16
EPS = 1e-06
NEG = -1000000000.0
THRESHOLDS = (12, 16, 23, 32, 46, 64, 91)
GELU_C = 0.7978845608028654
GELU_K = 0.044715
WIDE = pl.BlockSpec(memory_space=pltpu.VMEM)
SCALARS = pl.BlockSpec(memory_space=pltpu.SMEM)


def dot(left, right, left_dim, right_dim, precision=None):
    return lax.dot_general(
        left,
        right,
        (((left_dim,), (right_dim,)), ((), ())),
        preferred_element_type=F32,
        precision=precision,
    )


def code_of(delta):
    n = abs(delta)
    far = 8 + sum(1 for threshold in THRESHOLDS if n >= threshold)
    return (16 if delta > 0 else 0) + (n if n < 8 else far)


def code_block(size, distance):
    shape = (size, size)
    delta = (
        lax.broadcasted_iota(jnp.int32, shape, 0)
        - lax.broadcasted_iota(jnp.int32, shape, 1)
        + size * distance
    )
    n = jnp.abs(delta)
    far = jnp.full(shape, 8, jnp.int32)
    for threshold in THRESHOLDS:
        far = far + (n >= threshold).astype(jnp.int32)
    return jnp.where(delta > 0, 16, 0) + jnp.where(n < 8, n, far)


def codes_in(size, distance):
    return sorted(
        {code_of(size * distance + inner) for inner in range(1 - size, size)}
    )


def row_block(*shape):
    return pl.BlockSpec((1,) + shape, lambda r: (r,) + (0,) * len(shape))


def fixed(*shape):
    return pl.BlockSpec(shape, lambda r: (0,) * len(shape))


def cost(micros):
    return pl.CostEstimate(
        flops=int(micros * 1.1e9), bytes_accessed=int(micros * 1e6), transcendentals=0
    )


def shaped(shape, dtype):
    return jax.ShapeDtypeStruct(shape, dtype)


def norm_kernel(x_ref, gain_ref, out_ref):
    x = x_ref[0].astype(F32)
    scale = lax.rsqrt(jnp.mean(x * x, axis=-1, keepdims=True) + EPS)
    out_ref[0] = (x * scale * gain_ref[...]).astype(BF16)


def norm_one(hidden, gain):
    rows, size, width = hidden.shape
    return pl.pallas_call(
        norm_kernel,
        grid=(rows,),
        in_specs=[row_block(size, width), fixed(1, width)],
        out_specs=row_block(size, width),
        out_shape=shaped(hidden.shape, BF16),
        cost_estimate=cost(2),
        name="norm_one",
    )(hidden, gain)


def bias_kernel(parts, size, table_ref, out_ref):
    heads = out_ref.shape[0]
    for at in range(2 * parts - 1):
        distance = at - (parts - 1)
        present = codes_in(size, distance)
        codes = code_block(size, distance) if len(present) > 1 else None
        for head in range(heads):
            block = jnp.full((size, size), table_ref[head, present[0]], F32)
            for code in present[1:]:
                block = jnp.where(codes == code, table_ref[head, code], block)
            out_ref[head, at] = block


def bias_blocks(table, parts, size):
    heads = table.shape[0]
    return pl.pallas_call(
        functools.partial(bias_kernel, parts, size),
        in_specs=[SCALARS],
        out_specs=WIDE,
        out_shape=shaped((heads, 2 * parts - 1, size, size), F32),
        cost_estimate=cost(3),
        name="bias_blocks",
    )(table)


def chunk_bias(bias_ref, head, me, parts, first, count):
    return jnp.concatenate(
        [
            jnp.concatenate(
                [
                    bias_ref[head, (a_k ^ me) - (a_q ^ me) + parts - 1]
                    for a_q in range(first, first + count)
                ],
                axis=1,
            )
            for a_k in range(parts)
        ],
        axis=0,
    )


def chunk_valid(length, me, parts, size, count):
    inner = lax.broadcasted_iota(jnp.int32, (size, count * size), 0)
    return jnp.concatenate(
        [inner < length - (a_k ^ me) * size for a_k in range(parts)], axis=0
    )


def attend_kernel(
    heads,
    place_ref,
    length_ref,
    own_ref,
    pair_ref,
    far_low_ref,
    far_high_ref,
    last_low_ref,
    last_high_ref,
    query_ref,
    key_ref,
    value_ref,
    bias_ref,
    normed_ref,
    joint_ref,
    log_ref,
    *mixed_refs,
):
    parts = len(mixed_refs)
    size = own_ref.shape[1]
    me = place_ref[0]
    length = length_ref[pl.program_id(0)]
    normed_ref[0, 0:size] = own_ref[0]
    normed_ref[0, size : 2 * size] = pair_ref[0]
    normed_ref[0, 2 * size : 3 * size] = far_low_ref[0] + far_high_ref[0]
    normed_ref[0, 3 * size : 4 * size] = last_low_ref[0] + last_high_ref[0]
    inner = joint_ref.shape[1] // 3
    for part, ref in enumerate((query_ref, key_ref, value_ref)):
        joint_ref[0, part * inner : (part + 1) * inner] = dot(
            ref[...], normed_ref[0], 1, 1
        ).astype(BF16)
    head_size = inner // heads
    count = 2
    valid = chunk_valid(length, me, parts, size, count)
    for head in range(heads):
        low = head * head_size
        key = joint_ref[0, inner + low : inner + low + head_size, :]
        value = joint_ref[0, 2 * inner + low : 2 * inner + low + head_size, :]
        for first in range(0, parts, count):
            lanes = slice(first * size, (first + count) * size)
            query = joint_ref[0, low : low + head_size, lanes]
            scores = dot(key, query, 0, 0) + chunk_bias(
                bias_ref, head, me, parts, first, count
            )
            scores = jnp.where(valid, scores, NEG)
            peak = jnp.max(scores, axis=0, keepdims=True)
            raised = jnp.exp(scores - peak)
            total = jnp.sum(raised, axis=0, keepdims=True)
            mixed = (dot(value, raised.astype(BF16), 1, 0) / total).astype(BF16)
            for step in range(count):
                mixed_refs[first + step][0, low : low + head_size, :] = mixed[
                    :, step * size : (step + 1) * size
                ]
            log_ref[0, head : head + 1, lanes] = peak + jnp.log(total)


def attend(place, lengths, blocks, weights, bias, heads):
    rows, size, width = blocks[0].shape
    parts = (bias.shape[1] + 1) // 2
    full = parts * size
    inner = weights[0].shape[0]
    joint = 3 * inner
    return pl.pallas_call(
        functools.partial(attend_kernel, heads),
        grid=(rows,),
        in_specs=[SCALARS, SCALARS]
        + [row_block(size, width)] * 6
        + [fixed(inner, width)] * 3
        + [fixed(*bias.shape)],
        out_specs=[row_block(full, width), row_block(joint, full), row_block(heads, full)]
        + [row_block(inner, size)] * parts,
        out_shape=[
            shaped((rows, full, width), BF16),
            shaped((rows, joint, full), BF16),
            shaped((rows, heads, full), F32),
        ]
        + [shaped((rows, inner, size), BF16)] * parts,
        cost_estimate=cost(13),
        name="attend",
    )(place, lengths, *blocks, *weights, bias)


def middle_kernel(weight_ref, hidden_ref, gain_ref, *refs):
    mixed_refs, (middle_ref, normed_ref) = refs[:-2], refs[-2:]
    branch = sum(
        dot(ref[0], weight_ref[a], 0, 0) for a, ref in enumerate(mixed_refs)
    )
    middle = hidden_ref[0].astype(F32) + branch
    scale = lax.rsqrt(jnp.mean(middle * middle, axis=-1, keepdims=True) + EPS)
    middle_ref[0] = middle
    normed_ref[0] = (middle * scale * gain_ref[...]).astype(BF16)


def middle_of(gathered, hidden, gain, mixed):
    rows, size, width = hidden.shape
    inner = mixed[0].shape[1]
    return pl.pallas_call(
        middle_kernel,
        grid=(rows,),
        in_specs=[fixed(*gathered.shape), row_block(size, width), fixed(1, width)]
        + [row_block(inner, size)] * len(mixed),
        out_specs=[row_block(size, width)] * 2,
        out_shape=[shaped(hidden.shape, F32), shaped(hidden.shape, BF16)],
        cost_estimate=cost(4),
        name="middle_of",
    )(gathered, hidden, gain, *mixed)


def ffn_kernel(chained, *refs):
    normed_ref, grad_ref = refs[:2]
    in_refs, out_refs = refs[2:4], refs[4:6]
    gelu_ref, act_ref, branch_ref, back_ref, branch_sum, back_sum = refs[
        6 + chained :
    ]
    step = pl.program_id(0)
    normed = normed_ref[...]
    grad = grad_ref[...]
    branch = back = None
    for shard in range(2):
        weight_in = in_refs[shard][...]
        weight_out = out_refs[shard][...]
        v = dot(normed, weight_in, 1, 0)
        grad_gelu = dot(grad, weight_out, 1, 1).astype(BF16).astype(F32)
        square = v * v
        bent = jnp.tanh(GELU_C * (v + GELU_K * (square * v)))
        half = 0.5 * (1.0 + bent)
        gelu = (v * half).astype(BF16)
        slope = half + (0.5 * GELU_C) * v * (1.0 - bent * bent) * (
            1.0 + (3.0 * GELU_K) * square
        )
        grad_act = (grad_gelu * slope).astype(BF16)
        gelu_ref[shard] = gelu
        act_ref[shard] = grad_act
        more = dot(gelu, weight_out, 1, 0)
        more_back = dot(grad_act, weight_in, 1, 1)
        branch = more if branch is None else branch + more
        back = more_back if back is None else back + more_back

    @pl.when(step == 0)
    def _():
        branch_sum[...] = branch
        back_sum[...] = back

    @pl.when(step > 0)
    def _():
        branch_sum[...] += branch
        back_sum[...] += back

    @pl.when(step == pl.num_programs(0) - 1)
    def _():
        branch_ref[...] = branch_sum[...].astype(branch_ref.dtype)
        back_ref[...] = back_sum[...].astype(back_ref.dtype)


def feed_forward(normed, grad, w_in, w_out, other, half, kept, dtype):
    tokens, width = normed.shape
    units = w_in.shape[1]
    cut = 256 if units % 256 == 0 else units
    down = width // cut
    token_block = pl.BlockSpec((2, tokens, cut), lambda c: (0, half, c))
    in_specs = [
        fixed(tokens, width),
        fixed(tokens, width),
        pl.BlockSpec((width, cut), lambda c: (0, c)),
        pl.BlockSpec((width, cut), lambda c: (0, c)),
        pl.BlockSpec((cut, width), lambda c: (c, 0)),
        pl.BlockSpec((cut, width), lambda c: (c + down, 0)),
    ]
    args = [normed, grad, w_in, other, w_out, other]
    aliases = {}
    if kept is not None:
        in_specs += [pl.BlockSpec(memory_space=pl.ANY)] * 2
        args += list(kept)
        aliases = {6: 0, 7: 1}
    return pl.pallas_call(
        functools.partial(ffn_kernel, len(aliases)),
        grid=(units // cut,),
        in_specs=in_specs,
        out_specs=[token_block, token_block, fixed(tokens, width), fixed(tokens, width)],
        out_shape=[shaped((2, 2 * tokens, units), BF16)] * 2
        + [shaped((tokens, width), dtype)] * 2,
        scratch_shapes=[pltpu.VMEM((tokens, width), F32)] * 2,
        input_output_aliases=aliases,
        cost_estimate=cost(9),
        name="feed_forward",
    )(*args)


def middle_back_kernel(
    weight_ref,
    own_ref,
    other_ref,
    middle_ref,
    result_ref,
    gain_ref,
    grad_ref,
    low_ref,
    gain_grad_ref,
    *mixed_refs,
):
    back = own_ref[0] + other_ref[0].astype(F32)
    middle = middle_ref[0]
    scale = lax.rsqrt(jnp.mean(middle * middle, axis=-1, keepdims=True) + EPS)
    scaled = back * gain_ref[...]
    inner = jnp.mean(scaled * middle, axis=-1, keepdims=True)
    grad = result_ref[0] + scale * scaled - middle * (scale * scale * scale * inner)
    gain_grad = jnp.sum(back * (middle * scale), axis=0, keepdims=True)

    @pl.when(pl.program_id(0) == 0)
    def _():
        gain_grad_ref[...] = gain_grad

    @pl.when(pl.program_id(0) > 0)
    def _():
        gain_grad_ref[...] += gain_grad

    grad_ref[0] = grad
    low = grad.astype(BF16)
    low_ref[0] = low
    for a, ref in enumerate(mixed_refs):
        ref[0] = dot(weight_ref[a], low, 1, 1).astype(BF16)


def middle_back(gathered, own, other, middle, grad_result, gain):
    rows, size, width = middle.shape
    parts = gathered.shape[0]
    inner = gathered.shape[1]
    block = row_block(size, width)
    return pl.pallas_call(
        middle_back_kernel,
        grid=(rows,),
        in_specs=[fixed(*gathered.shape)] + [block] * 4 + [fixed(1, width)],
        out_specs=[block, block, fixed(1, width)] + [row_block(inner, size)] * parts,
        out_shape=[
            shaped(middle.shape, F32),
            shaped(middle.shape, BF16),
            shaped((1, width), F32),
        ]
        + [shaped((rows, inner, size), BF16)] * parts,
        cost_estimate=cost(5),
        name="middle_back",
    )(gathered, own, other, middle, grad_result, gain)


def attend_back_kernel(heads, parts, place_ref, length_ref, joint_ref, bias_ref, log_ref, *refs):
    mixed_refs = refs[:parts]
    joint_grads = refs[parts : 2 * parts]
    table_ref, sums = refs[2 * parts :]
    size = mixed_refs[0].shape[2]
    me = place_ref[0]
    row = pl.program_id(0)
    length = length_ref[row]
    inner = joint_ref.shape[1] // 3
    head_size = inner // heads
    count = 2

    @pl.when(row == 0)
    def _():
        sums[...] = jnp.zeros_like(sums)

    valid = chunk_valid(length, me, parts, size, count)
    for head in range(heads):
        low = head * head_size
        key = joint_ref[0, inner + low : inner + low + head_size, :]
        value = joint_ref[0, 2 * inner + low : 2 * inner + low + head_size, :]
        grad_key = grad_value = None
        for first in range(0, parts, count):
            lanes = slice(first * size, (first + count) * size)
            query = joint_ref[0, low : low + head_size, lanes]
            grad_mixed = jnp.concatenate(
                [mixed_refs[first + step][0, low : low + head_size, :] for step in range(count)],
                axis=1,
            )
            scores = dot(key, query, 0, 0) + chunk_bias(
                bias_ref, head, me, parts, first, count
            )
            probs = jnp.where(
                valid, jnp.exp(scores - log_ref[0, head : head + 1, lanes]), 0.0
            )
            grad_probs = dot(value, grad_mixed, 0, 0)
            inner_sum = jnp.sum(probs * grad_probs, axis=0, keepdims=True)
            grad_scores = probs * (grad_probs - inner_sum)
            low_scores = grad_scores.astype(BF16)
            more_value = dot(grad_mixed, probs.astype(BF16), 1, 1)
            more_key = dot(query, low_scores, 1, 1)
            grad_value = more_value if grad_value is None else grad_value + more_value
            grad_key = more_key if grad_key is None else grad_key + more_key
            grad_query = dot(key, low_scores, 1, 0).astype(BF16)
            for step in range(count):
                joint_grads[first + step][0, low : low + head_size, :] = grad_query[
                    :, step * size : (step + 1) * size
                ]
            for step in range(count):
                for a_k in range(parts):
                    at = (a_k ^ me) - ((first + step) ^ me) + parts - 1
                    sums[head, at] += grad_scores[
                        a_k * size : (a_k + 1) * size, step * size : (step + 1) * size
                    ]
        grad_key = grad_key.astype(BF16)
        grad_value = grad_value.astype(BF16)
        for a in range(parts):
            lanes = slice(a * size, (a + 1) * size)
            joint_grads[a][0, inner + low : inner + low + head_size, :] = grad_key[:, lanes]
            joint_grads[a][0, 2 * inner + low : 2 * inner + low + head_size, :] = grad_value[
                :, lanes
            ]

    @pl.when(row == pl.num_programs(0) - 1)
    def _():
        ones = jnp.ones((8, size), F32)
        for head in range(heads):
            lines = [jnp.zeros((1, size), F32)] * 32
            for at in range(2 * parts - 1):
                distance = at - (parts - 1)
                present = codes_in(size, distance)
                codes = code_block(size, distance) if len(present) > 1 else None
                block = sums[head, at]
                for code in present:
                    chosen = block if codes is None else jnp.where(codes == code, block, 0.0)
                    lines[code] = lines[code] + jnp.sum(chosen, axis=0, keepdims=True)
            lined = jnp.concatenate(lines + [jnp.zeros((size - 32, size), F32)], axis=0)
            table_ref[head] = dot(ones, lined, 1, 1, lax.Precision.HIGHEST)


def attend_back(place, lengths, joint, bias, logs, mixed):
    rows, wide, full = joint.shape
    parts = len(mixed)
    heads = bias.shape[0]
    inner, size = mixed[0].shape[1:]
    return pl.pallas_call(
        functools.partial(attend_back_kernel, heads, parts),
        grid=(rows,),
        in_specs=[
            SCALARS,
            SCALARS,
            row_block(wide, full),
            fixed(*bias.shape),
            row_block(heads, full),
        ]
        + [row_block(inner, size)] * parts,
        out_specs=[row_block(wide, size)] * parts + [fixed(heads, 8, size)],
        out_shape=[shaped((rows, wide, size), BF16)] * parts + [shaped((heads, 8, size), F32)],
        scratch_shapes=[pltpu.VMEM(bias.shape, F32)],
        cost_estimate=cost(15),
        name="attend_back",
    )(place, lengths, joint, bias, logs, *mixed)


def ffn_grad_kernel(normed_ref, normed_pair_ref, grad_ref, grad_pair_ref, gelu_ref, act_ref, out_ref):
    normed = jnp.concatenate((normed_ref[...], normed_pair_ref[...]), axis=0)
    grad = jnp.concatenate((grad_ref[...], grad_pair_ref[...]), axis=0)
    cuts = out_ref.shape[1]
    share = out_ref.shape[2] // 2
    for shard in range(2):
        for side, (left, right) in enumerate(
            ((normed, act_ref[shard]), (gelu_ref[shard], grad))
        ):
            total = dot(left, right, 0, 0).astype(BF16)
            for cut in range(cuts):
                out_ref[side, cut, shard * share : (shard + 1) * share] = total[
                    cut * share : (cut + 1) * share
                ]


def ffn_grad(normed, normed_pair, grad, grad_pair, gelu, act, copies):
    tokens, width = normed.shape
    units = gelu.shape[2]
    steps = 2
    share = (width + units) // copies
    return pl.pallas_call(
        ffn_grad_kernel,
        grid=(steps,),
        in_specs=[
            pl.BlockSpec((tokens, width // steps), lambda m: (0, m)),
            pl.BlockSpec((tokens, width // steps), lambda m: (0, m)),
            fixed(tokens, width),
            fixed(tokens, width),
            pl.BlockSpec((2, 2 * tokens, units // steps), lambda m: (0, 0, m)),
            fixed(2, 2 * tokens, units),
        ],
        out_specs=pl.BlockSpec(
            (2, copies // (2 * steps), 2 * share, width), lambda m: (0, m, 0, 0)
        ),
        out_shape=shaped((2, copies // 2, 2 * share, width), BF16),
        cost_estimate=cost(6),
        name="ffn_grad",
    )(normed, normed_pair, grad, grad_pair, gelu, act)


def joint_grad_kernel(
    parts, normed_ref, weight_ref, gain_ref, gain_two_ref, table_ref, branch_ref, *refs
):
    joint_grads = refs[:parts]
    mixed_refs = refs[parts : 2 * parts]
    out_ref, total, out_total = refs[2 * parts :]
    row = pl.program_id(0)
    grads = jnp.concatenate([ref[0] for ref in joint_grads], axis=1)
    mixed = jnp.concatenate([ref[0] for ref in mixed_refs], axis=0)
    more = dot(grads, normed_ref[0], 1, 0)
    more_out = dot(mixed, branch_ref[0], 1, 0)

    @pl.when(row == 0)
    def _():
        total[...] = more
        out_total[...] = more_out

    @pl.when(row > 0)
    def _():
        total[...] += more
        out_total[...] += more_out

    @pl.when(row == pl.num_programs(0) - 1)
    def _():
        wide, width = total.shape
        inner = mixed_refs[0].shape[1]
        cuts = out_ref.shape[0]
        gain_grad = (
            jnp.sum(total[...] * weight_ref[...].astype(F32), axis=0, keepdims=True)
            / gain_ref[...]
        )
        heads, _, size = table_ref.shape
        pad = jnp.zeros((1, width - size), F32)
        lines = [gain_grad, gain_two_ref[...]] + [
            jnp.concatenate([table_ref[head, 0:1], pad], axis=1) for head in range(heads)
        ]
        lines.append(jnp.zeros((8 - len(lines), width), F32))
        share, out_share = wide // cuts, inner // cuts
        for cut in range(cuts):
            out_ref[cut, 0:share] = total[cut * share : (cut + 1) * share].astype(BF16)
            at = share
            for a in range(parts):
                low = a * inner + cut * out_share
                out_ref[cut, at : at + out_share] = out_total[low : low + out_share].astype(BF16)
                at += out_share
            if cut == 0:
                out_ref[cut, at : at + 8] = jnp.concatenate(lines, axis=0).astype(BF16)
            else:
                out_ref[cut, at : at + 8] = jnp.zeros((8, width), BF16)


def joint_grad(
    normed, weights, gain, gain_two_grad, table_grad, grad_branch, joint_grads, mixed, copies
):
    rows, full, width = normed.shape
    wide, size = joint_grads[0].shape[1:]
    inner = mixed[0].shape[1]
    parts = len(joint_grads)
    cuts = copies if inner % (8 * copies) == 0 else 1
    length = (wide + parts * inner) // cuts + 8
    return pl.pallas_call(
        functools.partial(joint_grad_kernel, parts),
        grid=(rows,),
        in_specs=[
            row_block(full, width),
            fixed(wide, width),
            fixed(1, width),
            fixed(1, width),
            fixed(*table_grad.shape),
            row_block(size, width),
        ]
        + [row_block(wide, size)] * parts
        + [row_block(inner, size)] * parts,
        out_specs=fixed(cuts, length, width),
        out_shape=shaped((cuts, length, width), BF16),
        scratch_shapes=[pltpu.VMEM((wide, width), F32), pltpu.VMEM((parts * inner, width), F32)],
        cost_estimate=cost(6),
        name="joint_grad",
    )(normed, weights, gain, gain_two_grad, table_grad, grad_branch, *joint_grads, *mixed)


def recut(values, wide, parts, inner, copies):
    width = values.shape[2]
    whole = values[0]
    out = [whole[:wide].reshape(copies, -1, width)]
    for a in range(parts):
        low = wide + a * inner
        out.append(whole[low : low + inner].reshape(copies, -1, width))
    extra = whole[None, wide + parts * inner :]
    out.append(jnp.concatenate([extra] + [jnp.zeros_like(extra)] * (copies - 1), axis=0))
    return jnp.concatenate(out, axis=1)


def hidden_grad_kernel(place_ref, weight_ref, middle_ref, hidden_ref, gain_ref, *refs):
    joint_grads, out_ref = refs[:-1], refs[-1]
    me = place_ref[0]
    back = sum(dot(ref[0], weight_ref[a ^ me], 0, 0) for a, ref in enumerate(joint_grads))
    hidden = hidden_ref[0].astype(F32)
    scale = lax.rsqrt(jnp.mean(hidden * hidden, axis=-1, keepdims=True) + EPS)
    scaled = back * gain_ref[...]
    inner = jnp.mean(scaled * hidden, axis=-1, keepdims=True)
    out_ref[0] = middle_ref[0] + scale * scaled - hidden * (scale * scale * scale * inner)


def hidden_grad(place, gathered, grad_middle, hidden, gain, joint_grads):
    rows, size, width = hidden.shape
    wide = joint_grads[0].shape[1]
    block = row_block(size, width)
    return pl.pallas_call(
        hidden_grad_kernel,
        grid=(rows,),
        in_specs=[SCALARS, fixed(*gathered.shape), block, block, fixed(1, width)]
        + [row_block(wide, size)] * len(joint_grads),
        out_specs=block,
        out_shape=shaped(hidden.shape, F32),
        cost_estimate=cost(150),
        name="hidden_grad",
    )(place, gathered, grad_middle, hidden, gain, *joint_grads)


def after(values, *others):
    return lax.optimization_barrier((values, *others))[0]


def swap(values, distance):
    parts = lax.axis_size("tp")
    return lax.ppermute(values, "tp", [(i, i ^ distance) for i in range(parts)])


def swap_all(blocks):
    return [blocks[0]] + [swap(block, a) for a, block in enumerate(blocks) if a]


def gather_line(values, first, second):
    pair = swap(values, 1)
    inner = [(1, 2), (2, 1)]
    outer = [(1, 0), (2, 3)]
    last_low = lax.ppermute(values, "tp", inner)
    pair, last_low, *first = lax.optimization_barrier((pair, last_low, *first))
    far_low = lax.ppermute(pair, "tp", inner)
    far_high = lax.ppermute(last_low, "tp", outer)
    far_low, far_high, *second = lax.optimization_barrier((far_low, far_high, *second))
    last_high = lax.ppermute(far_low, "tp", outer)
    return [values, pair, far_low, far_high, last_low, last_high], first, second


def across(values, bit):
    count = lax.axis_size("dp")
    return lax.ppermute(values, "dp", [(i, i ^ (1 << bit)) for i in range(count)])


def dp_bits():
    return range(lax.axis_size("dp").bit_length() - 1)


def join(values):
    place = lax.axis_index("dp")
    for bit in dp_bits():
        upper = (place >> bit) & 1
        came = across(values, bit)
        values = jnp.where(
            upper == 1,
            jnp.concatenate((came, values), axis=0),
            jnp.concatenate((values, came), axis=0),
        )
    return values


def local(
    hidden_in,
    lengths,
    inst_lengths,
    w_query,
    w_key,
    w_value,
    attention_output_weight,
    feedforward_input_weight,
    feedforward_output_weight,
    rel_table,
    gain_attn,
    gain_ffn,
    grad_output,
    grad_pooled,
):
    rows, size, width = hidden_in.shape
    parts = lax.axis_size("tp")
    copies = lax.axis_size("dp")
    me = lax.axis_index("tp")
    group = lax.axis_index("dp")
    heads = rel_table.shape[1]
    inner = w_query.shape[1]
    tokens = rows * size
    place = me.astype(jnp.int32).reshape(1)
    gain_one = gain_attn.astype(F32).reshape(1, width)
    gain_two = gain_ffn.astype(F32).reshape(1, width)

    def share_of(weights):
        share = weights.shape[0] // copies
        return lax.dynamic_slice_in_dim(weights, group * share, share, 0)

    def fetched(shares, lead):
        everything = lax.all_gather(shares, "dp", axis=0, tiled=False)
        rest = everything[:, lead:].reshape(copies, parts, -1, width)
        return (
            jnp.swapaxes(rest, 0, 1).reshape(parts, -1, width),
            everything[:, :lead].reshape(-1, width),
        )

    first = norm_one(hidden_in, gain_one)
    attention_weights = jnp.concatenate(
        (w_query.T, w_key.T, w_value.T), axis=0
    )
    bias = bias_blocks(rel_table.T.astype(F32), parts, size)

    other_share = share_of(
        jnp.concatenate((feedforward_input_weight, feedforward_output_weight), axis=0)
    )
    ffn_share = other_share.shape[0]
    out_part = share_of(attention_output_weight)
    came_two = swap(jnp.concatenate((other_share, out_part), axis=0), 2)
    came_out = [out_part, swap(out_part, 1), swap(out_part, 3)]
    columns = grad_pooled.shape[1]
    spread = lax.dynamic_update_slice(
        jnp.zeros((rows, width), BF16), grad_pooled, (0, me * columns)
    )
    spread = swap_all([spread] * parts)
    blocks, (bias, came_two, *came_out), spread = gather_line(
        first, [bias, came_two] + came_out, spread
    )
    pool_cot = sum(block.astype(F32) for block in spread)
    counts = (lengths - inst_lengths).astype(F32)
    spots = me * size + jnp.arange(size, dtype=jnp.int32)
    mask = (
        (spots[None, :] >= inst_lengths[:, None]) & (spots[None, :] < lengths[:, None])
    ).astype(F32)
    grad_result = (
        grad_output.astype(F32)
        + pool_cot[:, None, :] * (mask / counts[:, None])[:, :, None]
    )
    grad_low = grad_result.astype(BF16).reshape(tokens, width)
    grad_low_pair = swap(grad_low, 1)


    shares = jnp.concatenate(
        [came_two[:ffn_share], *came_out[:2], came_two[ffn_share:], came_out[2]], axis=0
    )
    out_gathered, other_weights = fetched(shares, ffn_share)
    gathered = lax.all_gather(
        after(share_of(attention_weights), blocks[5]), ("tp", "dp"), axis=0, tiled=True
    ).reshape(parts, -1, width)
    normed, joint, logs, *mixed = attend(
        place, lengths, blocks, (w_query.T, w_key.T, w_value.T), bias, heads
    )
    mixed, grad_low_pair = lax.optimization_barrier((mixed, grad_low_pair))
    mixed = swap_all(mixed)
    middle, second = middle_of(out_gathered, hidden_in, gain_two, mixed)
    second = second.reshape(tokens, width)
    second_pair = swap(second, 1)

    gelu, grad_act, branch, back = feed_forward(
        second,
        grad_low,
        feedforward_input_weight,
        feedforward_output_weight,
        other_weights,
        0,
        None,
        F32,
    )
    gelu, grad_act, branch_pair, back_pair = feed_forward(
        second_pair,
        grad_low_pair,
        feedforward_input_weight,
        feedforward_output_weight,
        other_weights,
        1,
        (gelu, grad_act),
        BF16,
    )
    stacked = ffn_grad(
        second, second_pair, grad_low, grad_low_pair, gelu, grad_act, copies
    )
    summed = lax.psum_scatter(
        stacked.reshape(-1, width), "dp", scatter_dimension=0, tiled=True
    )

    back_came = after(swap(back_pair, 1), stacked, gathered)

    grad_middle, grad_branch, gain_two_grad, *grad_mixed = middle_back(
        out_gathered,
        back.reshape(rows, size, width),
        back_came.reshape(rows, size, width),
        middle,
        grad_result,
        gain_two,
    )
    grad_mixed = swap_all(grad_mixed)

    *joint_grads, table_grad = attend_back(place, lengths, joint, bias, logs, grad_mixed)
    came = swap_all(joint_grads)

    branch_came = swap(after(branch_pair, grad_mixed[-1]), 1)
    result = (
        middle
        + branch.reshape(rows, size, width)
        + branch_came.reshape(rows, size, width).astype(F32)
    )
    wide = 3 * inner
    heads_grad = joint_grad(
        normed,
        attention_weights,
        gain_one,
        gain_two_grad,
        table_grad,
        grad_branch,
        joint_grads,
        mixed,
        copies,
    )
    if heads_grad.shape[0] != copies:
        heads_grad = recut(heads_grad, wide, parts, inner, copies)
    mine = lax.psum_scatter(
        heads_grad.reshape(-1, width), "dp", scatter_dimension=0, tiled=True
    )
    summed = after(summed, heads_grad)
    own_sum = summed[:ffn_share].astype(F32) + swap(summed[ffn_share:], 2).astype(F32)
    whole_ffn = lax.all_gather(own_sum.astype(BF16), "dp", axis=0, tiled=True).astype(F32)
    grad_hidden = hidden_grad(
        place,
        gathered,
        grad_middle,
        hidden_in,
        gain_one,
        [after(came[0], heads_grad, own_sum, branch_came)] + came[1:],
    )
    mine, result = after((mine, result), grad_hidden)

    layer_out = result.astype(BF16)
    pool_part = jnp.sum(result * mask[:, :, None], axis=1) / counts[:, None]
    pool_sum = pool_part + sum(swap(pool_part, a) for a in range(1, parts))
    pooled = lax.dynamic_slice_in_dim(pool_sum, me * columns, columns, 1)
    share, out_share = wide // copies, inner // copies
    extra = mine[share + parts * out_share :]
    moved = swap_all(
        [
            jnp.concatenate(
                (mine[share + a * out_share : share + (a + 1) * out_share], extra), axis=0
            )
            for a in range(parts)
        ]
    )
    moved = sum(block.astype(F32) for block in moved)
    whole = join(
        jnp.concatenate(
            (
                mine[:share].astype(F32),
                moved[:out_share],
                moved[out_share : out_share + 2],
                extra[2:].astype(F32),
            ),
            axis=0,
        )[None].astype(BF16)
    )
    joint_sum = whole[:, :share].reshape(wide, width).astype(F32)
    whole_out = whole[:, share : share + out_share].reshape(inner, width).astype(F32)
    extra = whole[0, share + out_share :].astype(F32)
    table_sum = extra[2 : 2 + heads, : rel_table.shape[0]].T

    return (
        layer_out,
        pooled,
        grad_hidden,
        joint_sum[:inner].T,
        joint_sum[inner : 2 * inner].T,
        joint_sum[2 * inner : wide].T,
        whole_out,
        whole_ffn[:width],
        whole_ffn[width:],
        table_sum,
        extra[0],
        extra[1],
    )


def solution(mesh):
    in_specs = (
        P("dp", "tp", None),
        P("dp"),
        P("dp"),
        P(None, "tp"),
        P(None, "tp"),
        P(None, "tp"),
        P("tp", None),
        P(None, "tp"),
        P("tp", None),
        P(None, "tp"),
        P(),
        P(),
        P("dp", "tp", None),
        P("dp", "tp"),
    )
    out_specs = (
        P("dp", "tp", None),
        P("dp", "tp"),
        P("dp", "tp", None),
        P(None, "tp"),
        P(None, "tp"),
        P(None, "tp"),
        P("tp", None),
        P(None, "tp"),
        P("tp", None),
        P(None, "tp"),
        P(),
        P(),
    )
    return jax.shard_map(local, mesh=mesh, in_specs=in_specs, out_specs=out_specs, check_vma=False)
```

```python
import functools

import jax
import jax.numpy as jnp
from jax import lax
from jax.experimental import pallas as pl
from jax.experimental.pallas import tpu as pltpu
from jax.sharding import PartitionSpec as P

F32 = jnp.float32
BF16 = jnp.bfloat16
EPS = 1e-06
ROOM = 16 << 20
NEG = -1000000000.0
THRESHOLDS = (12, 16, 23, 32, 46, 64, 91)
GELU_C = 0.7978845608028654
GELU_K = 0.044715
WIDE = pl.BlockSpec(memory_space=pltpu.VMEM)
SCALARS = pl.BlockSpec(memory_space=pltpu.SMEM)


def dot(left, right, left_dim, right_dim, precision=None):
    return lax.dot_general(
        left,
        right,
        (((left_dim,), (right_dim,)), ((), ())),
        preferred_element_type=F32,
        precision=precision,
    )


def code_of(delta):
    n = abs(delta)
    far = 8 + sum(1 for threshold in THRESHOLDS if n >= threshold)
    return (16 if delta > 0 else 0) + (n if n < 8 else far)


def code_block(size, distance):
    shape = (size, size)
    delta = (
        lax.broadcasted_iota(jnp.int32, shape, 0)
        - lax.broadcasted_iota(jnp.int32, shape, 1)
        + size * distance
    )
    n = jnp.abs(delta)
    far = jnp.full(shape, 8, jnp.int32)
    for threshold in THRESHOLDS:
        far = far + (n >= threshold).astype(jnp.int32)
    return jnp.where(delta > 0, 16, 0) + jnp.where(n < 8, n, far)


def codes_in(size, distance):
    return sorted(
        {code_of(size * distance + inner) for inner in range(1 - size, size)}
    )


def cost(micros):
    return pl.CostEstimate(
        flops=int(micros * 1.1e9), bytes_accessed=int(micros * 1e6), transcendentals=0
    )


def shaped(shape, dtype):
    return jax.ShapeDtypeStruct(shape, dtype)


def near(values):
    return pltpu.with_memory_space_constraint(values, pltpu.VMEM)


def call(kernel, name, micros, rows, scalars, arrays, outs, scratch=()):
    def spec(shape, mark):
        if mark == "h":
            return pl.BlockSpec((1, *shape[1:]), lambda row: (row,) + (0,) * (len(shape) - 1))
        if mark == "w":
            return pl.BlockSpec(shape, lambda row: (0,) * len(shape))
        return WIDE

    marked = [(array if isinstance(array, tuple) else (array, "v")) for array in arrays]
    return pl.pallas_call(
        kernel,
        grid=(rows,),
        in_specs=[SCALARS] * len(scalars) + [spec(array.shape, mark) for array, mark in marked],
        out_specs=[spec(shape, mark) for shape, _, mark in outs],
        out_shape=[
            (pltpu.VMEM if mark == "v" else pltpu.HBM)(shape, dtype) for shape, dtype, mark in outs
        ],
        scratch_shapes=list(scratch),
        compiler_params=pltpu.CompilerParams(vmem_limit_bytes=ROOM),
        cost_estimate=cost(micros),
        name=name,
    )(
        *scalars,
        *[near(array) if mark == "v" else array for array, mark in marked],
    )


def turn():
    row = pl.program_id(0)
    return row, lambda ref: 0 if ref.shape[0] == 1 else row


def norm_kernel(x_ref, gain_ref, out_ref):
    gain = gain_ref[...]
    for row in range(x_ref.shape[0]):
        x = x_ref[row].astype(F32)
        scale = lax.rsqrt(jnp.mean(x * x, axis=-1, keepdims=True) + EPS)
        out_ref[row] = (x * scale * gain).astype(BF16)


def norm_one(hidden, gain):
    return call(norm_kernel, "norm_one", 2, 1, [], [hidden, gain], [(hidden.shape, BF16, "v")])[0]


def bias_kernel(parts, size, table_ref, out_ref):
    heads = out_ref.shape[0]
    for at in range(2 * parts - 1):
        distance = at - (parts - 1)
        present = codes_in(size, distance)
        codes = code_block(size, distance) if len(present) > 1 else None
        for head in range(heads):
            block = jnp.full((size, size), table_ref[head, present[0]], F32)
            for code in present[1:]:
                block = jnp.where(codes == code, table_ref[head, code], block)
            out_ref[head, at] = block


def bias_blocks(table, parts, size):
    heads = table.shape[0]
    return call(
        functools.partial(bias_kernel, parts, size),
        "bias_blocks",
        3,
        1,
        [table],
        [],
        [((heads, 2 * parts - 1, size, size), F32, "w")],
    )[0]


def chunk_bias(bias_ref, head, me, parts, first, count):
    return jnp.concatenate(
        [
            jnp.concatenate(
                [
                    bias_ref[head, (a_k ^ me) - (a_q ^ me) + parts - 1]
                    for a_q in range(first, first + count)
                ],
                axis=1,
            )
            for a_k in range(parts)
        ],
        axis=0,
    )


def chunk_valid(length, me, parts, size, count):
    inner = lax.broadcasted_iota(jnp.int32, (size, count * size), 0)
    return jnp.concatenate(
        [inner < length - (a_k ^ me) * size for a_k in range(parts)], axis=0
    )


def attend_kernel(
    heads,
    place_ref,
    length_ref,
    own_ref,
    pair_ref,
    far_low_ref,
    far_high_ref,
    last_low_ref,
    last_high_ref,
    query_ref,
    key_ref,
    value_ref,
    bias_ref,
    normed_ref,
    joint_ref,
    log_ref,
    *mixed_refs,
):
    parts = len(mixed_refs)
    size = own_ref.shape[1]
    me = place_ref[0]
    inner = joint_ref.shape[1] // 3
    head_size = inner // heads
    count = 2

    row, at = turn()
    out = at(normed_ref)
    normed_ref[out, 0:size] = own_ref[row]
    normed_ref[out, size : 2 * size] = pair_ref[row]
    normed_ref[out, 2 * size : 3 * size] = far_low_ref[row] + far_high_ref[row]
    normed_ref[out, 3 * size : 4 * size] = last_low_ref[row] + last_high_ref[row]
    for part, ref in enumerate((query_ref, key_ref, value_ref)):
        joint_ref[out, part * inner : (part + 1) * inner] = dot(
            ref[...], normed_ref[out], 1, 1
        ).astype(BF16)
    valid = chunk_valid(length_ref[row], me, parts, size, count)
    for head in range(heads):
        low = head * head_size
        key = joint_ref[out, inner + low : inner + low + head_size, :]
        value = joint_ref[out, 2 * inner + low : 2 * inner + low + head_size, :]
        for first in range(0, parts, count):
            lanes = slice(first * size, (first + count) * size)
            query = joint_ref[out, low : low + head_size, lanes]
            scores = dot(key, query, 0, 0) + chunk_bias(bias_ref, head, me, parts, first, count)
            scores = jnp.where(valid, scores, NEG)
            peak = jnp.max(scores, axis=0, keepdims=True)
            raised = jnp.exp(scores - peak)
            total = jnp.sum(raised, axis=0, keepdims=True)
            mixed = (dot(value, raised.astype(BF16), 1, 0) / total).astype(BF16)
            for step in range(count):
                mixed_refs[first + step][row, low : low + head_size, :] = mixed[
                    :, step * size : (step + 1) * size
                ]
            log_ref[out, head : head + 1, lanes] = peak + jnp.log(total)


def attend(place, lengths, blocks, weights, bias, heads):
    rows, size, width = blocks[0].shape
    parts = (bias.shape[1] + 1) // 2
    full = parts * size
    inner = weights[0].shape[0]
    return call(
        functools.partial(attend_kernel, heads),
        "attend",
        12,
        rows,
        [place, lengths],
        [*blocks, *weights, bias],
        [
            ((rows, full, width), BF16, "h"),
            ((rows, 3 * inner, full), BF16, "h"),
            ((rows, heads, full), F32, "h"),
        ]
        + [((rows, inner, size), BF16, "v")] * parts,
    )


def middle_kernel(weight_ref, hidden_ref, gain_ref, *refs):
    mixed_refs, (middle_ref, normed_ref, all_ref) = refs[:-3], refs[-3:]
    row, at = turn()
    mixed = jnp.concatenate([ref[row] for ref in mixed_refs], axis=0)
    all_ref[at(all_ref)] = mixed
    middle = hidden_ref[at(hidden_ref)].astype(F32) + dot(mixed, weight_ref[...], 0, 0)
    scale = lax.rsqrt(jnp.mean(middle * middle, axis=-1, keepdims=True) + EPS)
    middle_ref[at(middle_ref)] = middle
    normed_ref[row] = (middle * scale * gain_ref[...]).astype(BF16)


def middle_of(gathered, hidden, gain, mixed):
    rows, size, width = hidden.shape
    return call(
        middle_kernel,
        "middle_of",
        3,
        rows,
        [],
        [gathered, (hidden, "h"), gain, *mixed],
        [
            (hidden.shape, F32, "h"),
            (hidden.shape, BF16, "v"),
            ((rows, gathered.shape[0], size), BF16, "h"),
        ],
    )


def ffn_kernel(
    normed_ref,
    grad_ref,
    in_one_ref,
    in_two_ref,
    out_one_ref,
    out_two_ref,
    gelu_ref,
    act_ref,
    branch_ref,
    back_ref,
):
    shards = ((in_one_ref, out_one_ref), (in_two_ref, out_two_ref))
    for shard, (in_ref, out_ref) in enumerate(shards):
        v = dot(normed_ref[...], in_ref[...], 1, 0)
        grad_gelu = dot(grad_ref[...], out_ref[...], 1, 1).astype(BF16).astype(F32)
        square = v * v
        bent = jnp.tanh(GELU_C * (v + GELU_K * (square * v)))
        half = 0.5 * (1.0 + bent)
        slope = half + (0.5 * GELU_C) * v * (1.0 - bent * bent) * (
            1.0 + (3.0 * GELU_K) * square
        )
        gelu_ref[shard] = (v * half).astype(BF16)
        act_ref[shard] = (grad_gelu * slope).astype(BF16)
    back_ref[...] = sum(
        dot(act_ref[shard], in_ref[...], 1, 1) for shard, (in_ref, _) in enumerate(shards)
    ).astype(back_ref.dtype)
    branch_ref[...] = sum(
        dot(gelu_ref[shard], out_ref[...], 1, 0) for shard, (_, out_ref) in enumerate(shards)
    ).astype(branch_ref.dtype)


def feed_forward(normed, grad, w_in, w_out, other):
    tokens, width = normed.shape
    units = w_in.shape[1]
    return call(
        ffn_kernel,
        "feed_forward",
        6,
        1,
        [],
        [normed, grad, w_in, other[:width], w_out, other[width:]],
        [((2, tokens, units), BF16, "v")] * 2 + [((tokens, width), BF16, "w")] * 2,
    )


def middle_back_kernel(
    weight_ref,
    own_ref,
    other_ref,
    middle_ref,
    result_ref,
    gain_ref,
    grad_ref,
    low_ref,
    gain_grad_ref,
    *mixed_refs,
):
    row, at = turn()
    inner_size = mixed_refs[0].shape[1]
    back = own_ref[at(own_ref)].astype(F32) + other_ref[at(other_ref)].astype(F32)
    middle = middle_ref[at(middle_ref)]
    scale = lax.rsqrt(jnp.mean(middle * middle, axis=-1, keepdims=True) + EPS)
    scaled = back * gain_ref[...]
    inner = jnp.mean(scaled * middle, axis=-1, keepdims=True)
    grad = result_ref[at(result_ref)] + scale * scaled - middle * (scale * scale * scale * inner)
    gain_grad = jnp.sum(back * (middle * scale), axis=0, keepdims=True)

    @pl.when(row == 0)
    def _():
        gain_grad_ref[...] = gain_grad

    @pl.when(row > 0)
    def _():
        gain_grad_ref[...] += gain_grad

    grad_ref[at(grad_ref)] = grad
    low = grad.astype(BF16)
    low_ref[at(low_ref)] = low
    mixed = dot(weight_ref[...], low, 1, 1).astype(BF16)
    for a, ref in enumerate(mixed_refs):
        ref[row] = mixed[a * inner_size : (a + 1) * inner_size]


def middle_back(gathered, own, other, middle, grad_result, gain, parts):
    rows, size, width = middle.shape
    inner = gathered.shape[0] // parts
    return call(
        middle_back_kernel,
        "middle_back",
        4,
        rows,
        [],
        [gathered, (own, "h"), (other, "h"), (middle, "h"), (grad_result, "h"), gain],
        [(middle.shape, F32, "h"), (middle.shape, BF16, "h"), ((1, width), F32, "w")]
        + [((rows, inner, size), BF16, "v")] * parts,
    )


def attend_back_kernel(heads, parts, place_ref, length_ref, joint_ref, bias_ref, log_ref, *refs):
    mixed_refs = refs[:parts]
    joint_grads = refs[parts : 2 * parts]
    table_ref, sums = refs[2 * parts :]
    size = mixed_refs[0].shape[2]
    me = place_ref[0]
    inner = joint_ref.shape[1] // 3
    head_size = inner // heads
    count = 2
    row, at = turn()
    come = at(joint_ref)

    @pl.when(row == 0)
    def _():
        sums[...] = jnp.zeros_like(sums)

    valid = chunk_valid(length_ref[row], me, parts, size, count)
    for head in range(heads):
        low = head * head_size
        key_rows = slice(inner + low, inner + low + head_size)
        value_rows = slice(2 * inner + low, 2 * inner + low + head_size)
        key = joint_ref[come, key_rows, :]
        value = joint_ref[come, value_rows, :]
        grad_key = grad_value = None
        for first in range(0, parts, count):
            lanes = slice(first * size, (first + count) * size)
            query = joint_ref[come, low : low + head_size, lanes]
            grad_mixed = jnp.concatenate(
                [
                    mixed_refs[first + step][row, low : low + head_size, :]
                    for step in range(count)
                ],
                axis=1,
            )
            scores = dot(key, query, 0, 0) + chunk_bias(bias_ref, head, me, parts, first, count)
            probs = jnp.where(
                valid, jnp.exp(scores - log_ref[come, head : head + 1, lanes]), 0.0
            )
            grad_probs = dot(value, grad_mixed, 0, 0)
            inner_sum = jnp.sum(probs * grad_probs, axis=0, keepdims=True)
            grad_scores = probs * (grad_probs - inner_sum)
            low_scores = grad_scores.astype(BF16)
            more_value = dot(grad_mixed, probs.astype(BF16), 1, 1)
            more_key = dot(query, low_scores, 1, 1)
            grad_value = more_value if grad_value is None else grad_value + more_value
            grad_key = more_key if grad_key is None else grad_key + more_key
            grad_query = dot(key, low_scores, 1, 0).astype(BF16)
            for step in range(count):
                joint_grads[first + step][row, low : low + head_size, :] = grad_query[
                    :, step * size : (step + 1) * size
                ]
            for step in range(count):
                for a_k in range(parts):
                    place = (a_k ^ me) - ((first + step) ^ me) + parts - 1
                    sums[head, place] += grad_scores[
                        a_k * size : (a_k + 1) * size, step * size : (step + 1) * size
                    ]
        grad_key = grad_key.astype(BF16)
        grad_value = grad_value.astype(BF16)
        for a in range(parts):
            lanes = slice(a * size, (a + 1) * size)
            joint_grads[a][row, key_rows, :] = grad_key[:, lanes]
            joint_grads[a][row, value_rows, :] = grad_value[:, lanes]

    pl.when(row == pl.num_programs(0) - 1)(
        functools.partial(table_sums, heads, parts, size, sums, table_ref)
    )


def table_sums(heads, parts, size, sums, table_ref):
    ones = jnp.ones((8, size), F32)
    for head in range(heads):
        lines = [jnp.zeros((1, size), F32)] * 32
        for at in range(2 * parts - 1):
            distance = at - (parts - 1)
            present = codes_in(size, distance)
            codes = code_block(size, distance) if len(present) > 1 else None
            block = sums[head, at]
            for code in present:
                chosen = block if codes is None else jnp.where(codes == code, block, 0.0)
                lines[code] = lines[code] + jnp.sum(chosen, axis=0, keepdims=True)
        lined = jnp.concatenate(lines + [jnp.zeros((size - 32, size), F32)], axis=0)
        table_ref[head] = dot(ones, lined, 1, 1, lax.Precision.HIGHEST)


def attend_back(place, lengths, joint, bias, logs, mixed):
    rows, wide, full = joint.shape
    parts = len(mixed)
    heads = bias.shape[0]
    inner, size = mixed[0].shape[1:]
    return call(
        functools.partial(attend_back_kernel, heads, parts),
        "attend_back",
        14,
        rows,
        [place, lengths],
        [(joint, "h"), bias, (logs, "h"), *mixed],
        [((rows, wide, size), BF16, "v")] * parts + [((heads, 8, size), F32, "w")],
        [pltpu.VMEM(bias.shape, F32)],
    )


def ffn_grad_kernel(
    normed_ref,
    normed_pair_ref,
    grad_ref,
    grad_pair_ref,
    gelu_ref,
    gelu_pair_ref,
    act_ref,
    act_pair_ref,
    out_ref,
):
    half = pl.program_id(0)
    cuts = out_ref.shape[1]
    share = out_ref.shape[2] // 2
    size = cuts * share
    lanes = pl.ds(pl.multiple_of(half * size, size), size)
    normed = jnp.concatenate((normed_ref[:, lanes], normed_pair_ref[:, lanes]), axis=0)
    grad = jnp.concatenate((grad_ref[...], grad_pair_ref[...]), axis=0)
    for shard in range(2):
        act = jnp.concatenate((act_ref[shard], act_pair_ref[shard]), axis=0)
        gelu = jnp.concatenate(
            (gelu_ref[shard, :, lanes], gelu_pair_ref[shard, :, lanes]), axis=0
        )
        for side, (left, right) in enumerate(((normed, act), (gelu, grad))):
            total = dot(left, right, 0, 0).astype(BF16)
            for cut in range(cuts):
                out_ref[side, cut, shard * share : (shard + 1) * share] = total[
                    cut * share : (cut + 1) * share
                ]


def ffn_grad(arrays, copies):
    width, units = arrays[0].shape[1], arrays[4].shape[2]
    steps = 2
    share = (width + units) // copies
    return pl.pallas_call(
        ffn_grad_kernel,
        grid=(steps,),
        in_specs=[WIDE] * len(arrays),
        out_specs=pl.BlockSpec(
            (2, copies // (2 * steps), 2 * share, width), lambda m: (0, m, 0, 0)
        ),
        out_shape=pltpu.HBM((2, copies // 2, 2 * share, width), BF16),
        compiler_params=pltpu.CompilerParams(vmem_limit_bytes=ROOM),
        cost_estimate=cost(6),
        name="ffn_grad",
    )(*[near(array) for array in arrays])


def joint_grad_kernel(
    parts,
    normed_ref,
    query_ref,
    key_ref,
    value_ref,
    gain_ref,
    gain_two_ref,
    table_ref,
    branch_ref,
    mixed_ref,
    *refs,
):
    joint_grads = refs[:parts]
    out_ref, total, out_total = refs[parts:]
    row, at = turn()
    more = dot(
        jnp.concatenate([ref[row] for ref in joint_grads], axis=1), normed_ref[at(normed_ref)], 1, 0
    )
    more_out = dot(mixed_ref[at(mixed_ref)], branch_ref[at(branch_ref)], 1, 0)

    @pl.when(row == 0)
    def _():
        total[...] = more
        out_total[...] = more_out

    @pl.when(row > 0)
    def _():
        total[...] += more
        out_total[...] += more_out

    @pl.when(row == pl.num_programs(0) - 1)
    def _():
        width = out_ref.shape[2]
        wide = total.shape[0]
        inner = wide // 3
        cuts = out_ref.shape[0]
        gain_grad = (
            sum(
                jnp.sum(
                    total[part * inner : (part + 1) * inner] * ref[...].astype(F32),
                    axis=0,
                    keepdims=True,
                )
                for part, ref in enumerate((query_ref, key_ref, value_ref))
            )
            / gain_ref[...]
        )
        heads, _, size = table_ref.shape
        pad = jnp.zeros((1, width - size), F32)
        lines = [gain_grad, gain_two_ref[...]] + [
            jnp.concatenate([table_ref[head, 0:1], pad], axis=1) for head in range(heads)
        ]
        lines.append(jnp.zeros((8 - len(lines), width), F32))
        share, out_share = wide // cuts, inner // cuts
        for cut in range(cuts):
            out_ref[cut, 0:share] = total[cut * share : (cut + 1) * share].astype(BF16)
            low = share
            for a in range(parts):
                from_ = a * inner + cut * out_share
                out_ref[cut, low : low + out_share] = out_total[
                    from_ : from_ + out_share
                ].astype(BF16)
                low += out_share
            if cut == 0:
                out_ref[cut, low : low + 8] = jnp.concatenate(lines, axis=0).astype(BF16)
            else:
                out_ref[cut, low : low + 8] = jnp.zeros((8, width), BF16)


def joint_grad(
    normed, weights, gain, gain_two_grad, table_grad, grad_branch, joint_grads, mixed, copies
):
    rows, _, width = normed.shape
    wide = joint_grads[0].shape[1]
    inner = wide // 3
    parts = len(joint_grads)
    cuts = copies if inner % (8 * copies) == 0 else 1
    length = (wide + parts * inner) // cuts + 8
    return call(
        functools.partial(joint_grad_kernel, parts),
        "joint_grad",
        6,
        rows,
        [],
        [
            (normed, "h"),
            *weights,
            gain,
            (gain_two_grad, "w"),
            (table_grad, "w"),
            (grad_branch, "h"),
            (mixed, "h"),
            *joint_grads,
        ],
        [((cuts, length, width), BF16, "w")],
        [pltpu.VMEM((wide, width), F32), pltpu.VMEM((parts * inner, width), F32)],
    )[0]


def recut(values, wide, parts, inner, copies):
    width = values.shape[2]
    whole = values[0]
    out = [whole[:wide].reshape(copies, -1, width)]
    for a in range(parts):
        low = wide + a * inner
        out.append(whole[low : low + inner].reshape(copies, -1, width))
    extra = whole[None, wide + parts * inner :]
    out.append(jnp.concatenate([extra] + [jnp.zeros_like(extra)] * (copies - 1), axis=0))
    return jnp.concatenate(out, axis=1)


def hidden_grad_kernel(place_ref, weight_ref, middle_ref, hidden_ref, gain_ref, *refs):
    joint_grads, out_ref = refs[:-1], refs[-1]
    me = place_ref[0]
    row, at = turn()
    back = sum(dot(ref[row], weight_ref[a], 0, 0) for a, ref in enumerate(joint_grads))
    hidden = hidden_ref[at(hidden_ref)].astype(F32)
    scale = lax.rsqrt(jnp.mean(hidden * hidden, axis=-1, keepdims=True) + EPS)
    scaled = back * gain_ref[...]
    inner = jnp.mean(scaled * hidden, axis=-1, keepdims=True)
    out_ref[at(out_ref)] = (
        middle_ref[at(middle_ref)] + scale * scaled - hidden * (scale * scale * scale * inner)
    )


def hidden_grad(place, gathered, grad_middle, hidden, gain, joint_grads):
    return call(
        hidden_grad_kernel,
        "hidden_grad",
        150,
        hidden.shape[0],
        [place],
        [gathered, (grad_middle, "h"), (hidden, "h"), gain, *joint_grads],
        [(hidden.shape, F32, "h")],
    )[0]


def after(values, *others):
    return lax.optimization_barrier((values, *others))[0]


def swap(values, distance):
    parts = lax.axis_size("tp")
    return lax.ppermute(values, "tp", [(i, i ^ distance) for i in range(parts)])


def swap_all(blocks):
    return [blocks[0]] + [swap(block, a) for a, block in enumerate(blocks) if a]


def gather_line(values, first, second):
    pair = swap(values, 1)
    inner = [(1, 2), (2, 1)]
    outer = [(1, 0), (2, 3)]
    last_low = lax.ppermute(values, "tp", inner)
    pair, last_low, *first = lax.optimization_barrier((pair, last_low, *first))
    far_low = lax.ppermute(pair, "tp", inner)
    far_high = lax.ppermute(last_low, "tp", outer)
    far_low, far_high, *second = lax.optimization_barrier((far_low, far_high, *second))
    last_high = lax.ppermute(far_low, "tp", outer)
    return [values, pair, far_low, far_high, last_low, last_high], first, second


def across(values, bit):
    count = lax.axis_size("dp")
    return lax.ppermute(values, "dp", [(i, i ^ (1 << bit)) for i in range(count)])


def dp_bits():
    return range(lax.axis_size("dp").bit_length() - 1)


def join(values, other=None):
    place = lax.axis_index("dp")
    for bit in reversed(dp_bits()):
        upper = (place >> bit) & 1
        if bit == 0 and other is not None:
            values, other = lax.optimization_barrier((values, other))
        came = across(values, bit)
        values = jnp.where(
            upper == 1,
            jnp.concatenate((came, values), axis=0),
            jnp.concatenate((values, came), axis=0),
        )
    return values, other


def by_place(values):
    count = len(dp_bits())
    order = tuple(reversed(range(count))) + tuple(range(count, count + values.ndim - 1))
    return values.reshape((2,) * count + values.shape[1:]).transpose(order).reshape(values.shape)


def local(
    hidden_in,
    lengths,
    inst_lengths,
    w_query,
    w_key,
    w_value,
    attention_output_weight,
    feedforward_input_weight,
    feedforward_output_weight,
    rel_table,
    gain_attn,
    gain_ffn,
    grad_output,
    grad_pooled,
):
    rows, size, width = hidden_in.shape
    parts = lax.axis_size("tp")
    copies = lax.axis_size("dp")
    me = lax.axis_index("tp")
    group = lax.axis_index("dp")
    heads = rel_table.shape[1]
    inner = w_query.shape[1]
    tokens = rows * size
    place = me.astype(jnp.int32).reshape(1)
    gain_one = gain_attn.astype(F32).reshape(1, width)
    gain_two = gain_ffn.astype(F32).reshape(1, width)

    def share_of(weights):
        share = weights.shape[0] // copies
        return lax.dynamic_slice_in_dim(weights, group * share, share, 0)

    def fetched(shares, lead):
        everything = lax.all_gather(shares, "dp", axis=0, tiled=False)
        rest = everything[:, lead:].reshape(copies, parts, -1, width)
        return (
            jnp.swapaxes(rest, 0, 1).reshape(-1, width),
            everything[:, :lead].reshape(-1, width),
            everything,
        )

    first = norm_one(hidden_in, gain_one)
    attention_weights = jnp.concatenate(
        (w_query.T, w_key.T, w_value.T), axis=0
    )
    bias = bias_blocks(rel_table.T.astype(F32), parts, size)

    other_share = share_of(
        jnp.concatenate((feedforward_input_weight, feedforward_output_weight), axis=0)
    )
    ffn_share = other_share.shape[0]
    out_part = share_of(attention_output_weight)
    columns = grad_pooled.shape[1]
    spread = lax.dynamic_update_slice(
        jnp.zeros((rows, width), BF16), grad_pooled, (0, me * columns)
    )
    spread = swap_all([spread] * parts)
    blocks, (bias,), (out_part, other_share, *spread) = gather_line(
        first, [bias], [out_part, other_share] + spread
    )
    pool_cot = sum(block.astype(F32) for block in spread)
    counts = (lengths - inst_lengths).astype(F32)
    spots = me * size + jnp.arange(size, dtype=jnp.int32)
    mask = (
        (spots[None, :] >= inst_lengths[:, None]) & (spots[None, :] < lengths[:, None])
    ).astype(F32)
    grad_result = (
        grad_output.astype(F32)
        + pool_cot[:, None, :] * (mask / counts[:, None])[:, :, None]
    )
    grad_low = grad_result.astype(BF16).reshape(tokens, width)

    came = swap_all([out_part, out_part, jnp.concatenate((out_part, other_share), axis=0), out_part])
    out_size = out_part.shape[0]
    out_gathered, other_weights, _ = fetched(
        after(
            jnp.concatenate([came[2][out_size:]] + [block[:out_size] for block in came], axis=0),
            blocks[5],
        ),
        ffn_share,
    )
    blocks[5], grad_low = lax.optimization_barrier((blocks[5], grad_low))
    grad_low_pair = swap(grad_low, 1)
    came_joint = jnp.concatenate(
        swap_all([after(share_of(attention_weights), blocks[5])] * parts), axis=0
    )
    normed, joint, logs, *mixed = attend(
        place, lengths, blocks, (w_query.T, w_key.T, w_value.T), bias, heads
    )
    mixed, grad_low_pair, came_joint = lax.optimization_barrier((mixed, grad_low_pair, came_joint))
    gathered, _, joint_there = fetched(came_joint, 0)
    gathered = gathered.reshape(parts, -1, width)
    mixed = swap_all(mixed)
    middle, second, mixed = middle_of(out_gathered, hidden_in, gain_two, mixed)
    second = second.reshape(tokens, width)
    second_pair = swap(second, 1)

    weights = (feedforward_input_weight, feedforward_output_weight, other_weights)
    gelu, act, branch, back = feed_forward(second, grad_low, *weights)
    gelu_pair, act_pair, branch_pair, back_pair = feed_forward(
        second_pair, grad_low_pair, *weights
    )

    stacked = ffn_grad(
        (second, second_pair, grad_low, grad_low_pair, gelu, gelu_pair, act, act_pair), copies
    )
    summed = lax.psum_scatter(
        after(stacked, joint_there).reshape(-1, width), "dp", scatter_dimension=0, tiled=True
    )

    back_came = after(swap(back_pair, 1), stacked)

    grad_middle, grad_branch, gain_two_grad, *grad_mixed = middle_back(
        out_gathered,
        back.reshape(rows, size, width),
        back_came.reshape(rows, size, width),
        middle,
        grad_result,
        gain_two,
        parts,
    )
    grad_mixed = swap_all(grad_mixed)

    *joint_grads, table_grad = attend_back(place, lengths, joint, bias, logs, grad_mixed)
    came = swap_all(joint_grads)

    branch_came = swap(after(branch_pair, grad_mixed[-1]), 1)
    result = (
        middle
        + branch.reshape(rows, size, width).astype(F32)
        + branch_came.reshape(rows, size, width).astype(F32)
    )
    wide = 3 * inner
    heads_grad = joint_grad(
        normed,
        (w_query.T, w_key.T, w_value.T),
        gain_one,
        gain_two_grad,
        table_grad,
        grad_branch,
        joint_grads,
        mixed,
        copies,
    )
    if heads_grad.shape[0] != copies:
        heads_grad = recut(heads_grad, wide, parts, inner, copies)
    mine = lax.psum_scatter(
        heads_grad.reshape(-1, width), "dp", scatter_dimension=0, tiled=True
    )
    summed = after(summed, heads_grad)
    own_sum = summed[:ffn_share].astype(F32) + swap(summed[ffn_share:], 2).astype(F32)
    whole_ffn = lax.all_gather(own_sum.astype(BF16), "dp", axis=0, tiled=True).astype(F32)
    grad_hidden = hidden_grad(
        place,
        gathered,
        grad_middle,
        hidden_in,
        gain_one,
        [after(came[0], heads_grad, own_sum, branch_came)] + came[1:],
    )
    mine, result = after((mine, result), grad_hidden)

    layer_out = result.astype(BF16)
    pool_part = jnp.sum(result * mask[:, :, None], axis=1) / counts[:, None]
    pool_sum = pool_part + sum(swap(pool_part, a) for a in range(1, parts))
    pooled = lax.dynamic_slice_in_dim(pool_sum, me * columns, columns, 1)
    share, out_share = wide // copies, inner // copies
    extra = mine[share + parts * out_share :]
    moved = swap_all(
        [
            jnp.concatenate(
                (mine[share + a * out_share : share + (a + 1) * out_share], extra), axis=0
            )
            for a in range(parts)
        ]
    )
    moved = sum(block.astype(F32) for block in moved)
    whole, _ = join(
        jnp.concatenate(
            (
                mine[:share].astype(F32),
                moved[:out_share],
                moved[out_share : out_share + 2],
                extra[2:].astype(F32),
            ),
            axis=0,
        )[None].astype(BF16)
    )
    joint_sum = by_place(whole[:, :share]).reshape(wide, width).astype(F32)
    whole_out = by_place(whole[:, share : share + out_share]).reshape(inner, width).astype(F32)
    extra = whole[0, share + out_share :].astype(F32)
    table_sum = extra[2 : 2 + heads, : rel_table.shape[0]].T

    return (
        layer_out,
        pooled,
        grad_hidden,
        joint_sum[:inner].T,
        joint_sum[inner : 2 * inner].T,
        joint_sum[2 * inner : wide].T,
        whole_out,
        whole_ffn[:width],
        whole_ffn[width:],
        table_sum,
        extra[0],
        extra[1],
    )


def solution(mesh):
    in_specs = (
        P("dp", "tp", None),
        P("dp"),
        P("dp"),
        P(None, "tp"),
        P(None, "tp"),
        P(None, "tp"),
        P("tp", None),
        P(None, "tp"),
        P("tp", None),
        P(None, "tp"),
        P(),
        P(),
        P("dp", "tp", None),
        P("dp", "tp"),
    )
    out_specs = (
        P("dp", "tp", None),
        P("dp", "tp"),
        P("dp", "tp", None),
        P(None, "tp"),
        P(None, "tp"),
        P(None, "tp"),
        P("tp", None),
        P(None, "tp"),
        P("tp", None),
        P(None, "tp"),
        P(),
        P(),
    )
    return jax.shard_map(local, mesh=mesh, in_specs=in_specs, out_specs=out_specs, check_vma=False)
```

```python
import functools

import jax
import jax.numpy as jnp
from jax import lax
from jax.experimental import pallas as pl
from jax.experimental.pallas import tpu as pltpu
from jax.sharding import PartitionSpec as P

F32 = jnp.float32
BF16 = jnp.bfloat16
EPS = 1e-06
ROOM = 16 << 20
NEG = -1000000000.0
THRESHOLDS = (12, 16, 23, 32, 46, 64, 91)
GELU_C = 0.7978845608028654
GELU_K = 0.044715
WIDE = pl.BlockSpec(memory_space=pltpu.VMEM)
SCALARS = pl.BlockSpec(memory_space=pltpu.SMEM)


def dot(left, right, left_dim, right_dim, precision=None):
    return lax.dot_general(
        left,
        right,
        (((left_dim,), (right_dim,)), ((), ())),
        preferred_element_type=F32,
        precision=precision,
    )


def code_of(delta):
    n = abs(delta)
    far = 8 + sum(1 for threshold in THRESHOLDS if n >= threshold)
    return (16 if delta > 0 else 0) + (n if n < 8 else far)


def code_block(size, distance):
    shape = (size, size)
    delta = (
        lax.broadcasted_iota(jnp.int32, shape, 0)
        - lax.broadcasted_iota(jnp.int32, shape, 1)
        + size * distance
    )
    n = jnp.abs(delta)
    far = jnp.full(shape, 8, jnp.int32)
    for threshold in THRESHOLDS:
        far = far + (n >= threshold).astype(jnp.int32)
    return jnp.where(delta > 0, 16, 0) + jnp.where(n < 8, n, far)


def codes_in(size, distance):
    return sorted(
        {code_of(size * distance + inner) for inner in range(1 - size, size)}
    )


def cost(micros):
    return pl.CostEstimate(
        flops=int(micros * 1.1e9), bytes_accessed=int(micros * 1e6), transcendentals=0
    )


def shaped(shape, dtype):
    return jax.ShapeDtypeStruct(shape, dtype)


def near(values):
    return pltpu.with_memory_space_constraint(values, pltpu.VMEM)


def call(kernel, name, micros, rows, scalars, arrays, outs, scratch=()):
    def spec(shape, mark):
        if mark == "h":
            return pl.BlockSpec((1, *shape[1:]), lambda row: (row,) + (0,) * (len(shape) - 1))
        if mark == "w":
            return pl.BlockSpec(shape, lambda row: (0,) * len(shape))
        return WIDE

    marked = [(array if isinstance(array, tuple) else (array, "v")) for array in arrays]
    return pl.pallas_call(
        kernel,
        grid=(rows,),
        in_specs=[SCALARS] * len(scalars) + [spec(array.shape, mark) for array, mark in marked],
        out_specs=[spec(shape, mark) for shape, _, mark in outs],
        out_shape=[
            (pltpu.VMEM if mark == "v" else pltpu.HBM)(shape, dtype) for shape, dtype, mark in outs
        ],
        scratch_shapes=list(scratch),
        compiler_params=pltpu.CompilerParams(vmem_limit_bytes=ROOM),
        cost_estimate=cost(micros),
        name=name,
    )(
        *scalars,
        *[near(array) if mark == "v" else array for array, mark in marked],
    )


def turn():
    row = pl.program_id(0)
    return row, lambda ref: 0 if ref.shape[0] == 1 else row


def norm_kernel(x_ref, gain_ref, out_ref):
    gain = gain_ref[...]
    for row in range(x_ref.shape[0]):
        x = x_ref[row].astype(F32)
        scale = lax.rsqrt(jnp.mean(x * x, axis=-1, keepdims=True) + EPS)
        out_ref[row] = (x * scale * gain).astype(BF16)


def norm_one(hidden, gain):
    return call(norm_kernel, "norm_one", 2, 1, [], [hidden, gain], [(hidden.shape, BF16, "v")])[0]


def bias_kernel(parts, size, table_ref, out_ref):
    heads = out_ref.shape[0]
    for at in range(2 * parts - 1):
        distance = at - (parts - 1)
        present = codes_in(size, distance)
        codes = code_block(size, distance) if len(present) > 1 else None
        for head in range(heads):
            block = jnp.full((size, size), table_ref[head, present[0]], F32)
            for code in present[1:]:
                block = jnp.where(codes == code, table_ref[head, code], block)
            out_ref[head, at] = block


def bias_blocks(table, parts, size):
    heads = table.shape[0]
    return call(
        functools.partial(bias_kernel, parts, size),
        "bias_blocks",
        3,
        1,
        [table],
        [],
        [((heads, 2 * parts - 1, size, size), F32, "w")],
    )[0]


def chunk_bias(bias_ref, head, me, parts, first, count):
    return jnp.concatenate(
        [
            jnp.concatenate(
                [
                    bias_ref[head, (a_k ^ me) - (a_q ^ me) + parts - 1]
                    for a_q in range(first, first + count)
                ],
                axis=1,
            )
            for a_k in range(parts)
        ],
        axis=0,
    )


def chunk_valid(length, me, parts, size, count):
    inner = lax.broadcasted_iota(jnp.int32, (size, count * size), 0)
    return jnp.concatenate(
        [inner < length - (a_k ^ me) * size for a_k in range(parts)], axis=0
    )


def attend_kernel(
    heads,
    place_ref,
    length_ref,
    own_ref,
    pair_ref,
    far_low_ref,
    far_high_ref,
    last_low_ref,
    last_high_ref,
    query_ref,
    key_ref,
    value_ref,
    bias_ref,
    normed_ref,
    joint_ref,
    log_ref,
    *mixed_refs,
):
    parts = len(mixed_refs)
    size = own_ref.shape[1]
    me = place_ref[0]
    inner = joint_ref.shape[1] // 3
    head_size = inner // heads
    count = parts

    row, at = turn()
    out = at(normed_ref)
    normed_ref[out, 0:size] = own_ref[row]
    normed_ref[out, size : 2 * size] = pair_ref[row]
    normed_ref[out, 2 * size : 3 * size] = far_low_ref[row] + far_high_ref[row]
    normed_ref[out, 3 * size : 4 * size] = last_low_ref[row] + last_high_ref[row]
    for part, ref in enumerate((query_ref, key_ref, value_ref)):
        joint_ref[out, part * inner : (part + 1) * inner] = dot(
            ref[...], normed_ref[out], 1, 1
        ).astype(BF16)
    valid = chunk_valid(length_ref[row], me, parts, size, count)
    spans = [slice(head * head_size, (head + 1) * head_size) for head in range(heads)]
    scores = [
        dot(joint_ref[out, inner + span.start : inner + span.stop, :], joint_ref[out, span, :], 0, 0)
        for span in spans
    ]
    for head, span in enumerate(spans):
        biased = scores[head] + chunk_bias(bias_ref, head, me, parts, 0, parts)
        biased = jnp.where(valid, biased, NEG)
        peak = jnp.max(biased, axis=0, keepdims=True)
        raised = jnp.exp(biased - peak)
        total = jnp.sum(raised, axis=0, keepdims=True)
        scores[head] = (raised.astype(BF16), total)
        log_ref[out, head : head + 1, :] = peak + jnp.log(total)
    for head, span in enumerate(spans):
        raised, total = scores[head]
        value = joint_ref[out, 2 * inner + span.start : 2 * inner + span.stop, :]
        mixed = (dot(value, raised, 1, 0) / total).astype(BF16)
        for step in range(parts):
            mixed_refs[step][row, span, :] = mixed[:, step * size : (step + 1) * size]


def attend(place, lengths, blocks, weights, bias, heads):
    rows, size, width = blocks[0].shape
    parts = (bias.shape[1] + 1) // 2
    full = parts * size
    inner = weights[0].shape[0]
    return call(
        functools.partial(attend_kernel, heads),
        "attend",
        12,
        rows,
        [place, lengths],
        [*blocks, *weights, bias],
        [
            ((rows, full, width), BF16, "h"),
            ((rows, 3 * inner, full), BF16, "h"),
            ((rows, heads, full), F32, "h"),
        ]
        + [((rows, inner, size), BF16, "v")] * parts,
    )


def middle_kernel(weight_ref, hidden_ref, gain_ref, *refs):
    mixed_refs, (middle_ref, normed_ref, all_ref) = refs[:-3], refs[-3:]
    row, at = turn()
    mixed = jnp.concatenate([ref[row] for ref in mixed_refs], axis=0)
    all_ref[at(all_ref)] = mixed
    middle = hidden_ref[at(hidden_ref)].astype(F32) + dot(mixed, weight_ref[...], 0, 0)
    scale = lax.rsqrt(jnp.mean(middle * middle, axis=-1, keepdims=True) + EPS)
    middle_ref[at(middle_ref)] = middle
    normed_ref[row] = (middle * scale * gain_ref[...]).astype(BF16)


def middle_of(gathered, hidden, gain, mixed):
    rows, size, width = hidden.shape
    return call(
        middle_kernel,
        "middle_of",
        3,
        rows,
        [],
        [gathered, (hidden, "h"), gain, *mixed],
        [
            (hidden.shape, F32, "h"),
            (hidden.shape, BF16, "v"),
            ((rows, gathered.shape[0], size), BF16, "h"),
        ],
    )


def ffn_kernel(
    normed_ref,
    grad_ref,
    in_one_ref,
    in_two_ref,
    out_one_ref,
    out_two_ref,
    gelu_ref,
    act_ref,
    branch_ref,
    back_ref,
):
    shards = ((in_one_ref, out_one_ref), (in_two_ref, out_two_ref))
    for shard, (in_ref, out_ref) in enumerate(shards):
        v = dot(normed_ref[...], in_ref[...], 1, 0)
        grad_gelu = dot(grad_ref[...], out_ref[...], 1, 1).astype(BF16).astype(F32)
        square = v * v
        bent = jnp.tanh(GELU_C * (v + GELU_K * (square * v)))
        half = 0.5 * (1.0 + bent)
        slope = half + (0.5 * GELU_C) * v * (1.0 - bent * bent) * (
            1.0 + (3.0 * GELU_K) * square
        )
        gelu_ref[shard] = (v * half).astype(BF16)
        act_ref[shard] = (grad_gelu * slope).astype(BF16)
    back_ref[...] = sum(
        dot(act_ref[shard], in_ref[...], 1, 1) for shard, (in_ref, _) in enumerate(shards)
    ).astype(back_ref.dtype)
    branch_ref[...] = sum(
        dot(gelu_ref[shard], out_ref[...], 1, 0) for shard, (_, out_ref) in enumerate(shards)
    ).astype(branch_ref.dtype)


def feed_forward(normed, grad, w_in, w_out, other):
    tokens, width = normed.shape
    units = w_in.shape[1]
    return call(
        ffn_kernel,
        "feed_forward",
        6,
        1,
        [],
        [normed, grad, w_in, other[:width], w_out, other[width:]],
        [((2, tokens, units), BF16, "v")] * 2 + [((tokens, width), BF16, "w")] * 2,
    )


def middle_back_kernel(
    weight_ref,
    own_ref,
    other_ref,
    middle_ref,
    result_ref,
    gain_ref,
    grad_ref,
    low_ref,
    gain_grad_ref,
    *mixed_refs,
):
    row, at = turn()
    inner_size = mixed_refs[0].shape[1]
    back = own_ref[at(own_ref)].astype(F32) + other_ref[at(other_ref)].astype(F32)
    middle = middle_ref[at(middle_ref)]
    scale = lax.rsqrt(jnp.mean(middle * middle, axis=-1, keepdims=True) + EPS)
    scaled = back * gain_ref[...]
    inner = jnp.mean(scaled * middle, axis=-1, keepdims=True)
    grad = result_ref[at(result_ref)] + scale * scaled - middle * (scale * scale * scale * inner)
    gain_grad = jnp.sum(back * (middle * scale), axis=0, keepdims=True)

    @pl.when(row == 0)
    def _():
        gain_grad_ref[...] = gain_grad

    @pl.when(row > 0)
    def _():
        gain_grad_ref[...] += gain_grad

    grad_ref[at(grad_ref)] = grad
    low = grad.astype(BF16)
    low_ref[at(low_ref)] = low
    mixed = dot(weight_ref[...], low, 1, 1).astype(BF16)
    for a, ref in enumerate(mixed_refs):
        ref[row] = mixed[a * inner_size : (a + 1) * inner_size]


def middle_back(gathered, own, other, middle, grad_result, gain, parts):
    rows, size, width = middle.shape
    inner = gathered.shape[0] // parts
    return call(
        middle_back_kernel,
        "middle_back",
        4,
        rows,
        [],
        [gathered, (own, "h"), (other, "h"), (middle, "h"), (grad_result, "h"), gain],
        [(middle.shape, F32, "h"), (middle.shape, BF16, "h"), ((1, width), F32, "w")]
        + [((rows, inner, size), BF16, "v")] * parts,
    )


def attend_back_kernel(heads, parts, place_ref, length_ref, joint_ref, bias_ref, log_ref, *refs):
    mixed_refs = refs[:parts]
    joint_grads = refs[parts : 2 * parts]
    table_ref, sums = refs[2 * parts :]
    size = mixed_refs[0].shape[2]
    me = place_ref[0]
    inner = joint_ref.shape[1] // 3
    head_size = inner // heads
    count = parts
    row, at = turn()
    come = at(joint_ref)

    @pl.when(row == 0)
    def _():
        sums[...] = jnp.zeros_like(sums)

    valid = chunk_valid(length_ref[row], me, parts, size, count)
    for head in range(heads):
        low = head * head_size
        key_rows = slice(inner + low, inner + low + head_size)
        value_rows = slice(2 * inner + low, 2 * inner + low + head_size)
        key = joint_ref[come, key_rows, :]
        value = joint_ref[come, value_rows, :]
        grad_key = grad_value = None
        for first in range(0, parts, count):
            lanes = slice(first * size, (first + count) * size)
            query = joint_ref[come, low : low + head_size, lanes]
            grad_mixed = jnp.concatenate(
                [
                    mixed_refs[first + step][row, low : low + head_size, :]
                    for step in range(count)
                ],
                axis=1,
            )
            scores = dot(key, query, 0, 0) + chunk_bias(bias_ref, head, me, parts, first, count)
            probs = jnp.where(
                valid, jnp.exp(scores - log_ref[come, head : head + 1, lanes]), 0.0
            )
            grad_probs = dot(value, grad_mixed, 0, 0)
            inner_sum = jnp.sum(probs * grad_probs, axis=0, keepdims=True)
            grad_scores = probs * (grad_probs - inner_sum)
            low_scores = grad_scores.astype(BF16)
            more_value = dot(grad_mixed, probs.astype(BF16), 1, 1)
            more_key = dot(query, low_scores, 1, 1)
            grad_value = more_value if grad_value is None else grad_value + more_value
            grad_key = more_key if grad_key is None else grad_key + more_key
            grad_query = dot(key, low_scores, 1, 0).astype(BF16)
            for step in range(count):
                joint_grads[first + step][row, low : low + head_size, :] = grad_query[
                    :, step * size : (step + 1) * size
                ]
            for step in range(count):
                for a_k in range(parts):
                    place = (a_k ^ me) - ((first + step) ^ me) + parts - 1
                    sums[head, place] += grad_scores[
                        a_k * size : (a_k + 1) * size, step * size : (step + 1) * size
                    ]
        grad_key = grad_key.astype(BF16)
        grad_value = grad_value.astype(BF16)
        for a in range(parts):
            lanes = slice(a * size, (a + 1) * size)
            joint_grads[a][row, key_rows, :] = grad_key[:, lanes]
            joint_grads[a][row, value_rows, :] = grad_value[:, lanes]

    pl.when(row == pl.num_programs(0) - 1)(
        functools.partial(table_sums, heads, parts, size, sums, table_ref)
    )


def table_sums(heads, parts, size, sums, table_ref):
    ones = jnp.ones((8, size), F32)
    for head in range(heads):
        lines = [jnp.zeros((1, size), F32)] * 32
        for at in range(2 * parts - 1):
            distance = at - (parts - 1)
            present = codes_in(size, distance)
            codes = code_block(size, distance) if len(present) > 1 else None
            block = sums[head, at]
            for code in present:
                chosen = block if codes is None else jnp.where(codes == code, block, 0.0)
                lines[code] = lines[code] + jnp.sum(chosen, axis=0, keepdims=True)
        lined = jnp.concatenate(lines + [jnp.zeros((size - 32, size), F32)], axis=0)
        table_ref[head] = dot(ones, lined, 1, 1, lax.Precision.HIGHEST)


def attend_back(place, lengths, joint, bias, logs, mixed):
    rows, wide, full = joint.shape
    parts = len(mixed)
    heads = bias.shape[0]
    inner, size = mixed[0].shape[1:]
    return call(
        functools.partial(attend_back_kernel, heads, parts),
        "attend_back",
        14,
        rows,
        [place, lengths],
        [(joint, "h"), bias, (logs, "h"), *mixed],
        [((rows, wide, size), BF16, "v")] * parts + [((heads, 8, size), F32, "w")],
        [pltpu.VMEM(bias.shape, F32)],
    )


def ffn_grad_kernel(
    normed_ref,
    normed_pair_ref,
    grad_ref,
    grad_pair_ref,
    gelu_ref,
    gelu_pair_ref,
    act_ref,
    act_pair_ref,
    out_ref,
):
    half = pl.program_id(0)
    cuts = out_ref.shape[1]
    share = out_ref.shape[2] // 2
    size = cuts * share
    lanes = pl.ds(pl.multiple_of(half * size, size), size)
    normed = jnp.concatenate((normed_ref[:, lanes], normed_pair_ref[:, lanes]), axis=0)
    grad = jnp.concatenate((grad_ref[...], grad_pair_ref[...]), axis=0)
    for shard in range(2):
        act = jnp.concatenate((act_ref[shard], act_pair_ref[shard]), axis=0)
        gelu = jnp.concatenate(
            (gelu_ref[shard, :, lanes], gelu_pair_ref[shard, :, lanes]), axis=0
        )
        for side, (left, right) in enumerate(((normed, act), (gelu, grad))):
            total = dot(left, right, 0, 0).astype(BF16)
            for cut in range(cuts):
                out_ref[side, cut, shard * share : (shard + 1) * share] = total[
                    cut * share : (cut + 1) * share
                ]


def ffn_grad(arrays, copies):
    width, units = arrays[0].shape[1], arrays[4].shape[2]
    steps = 2
    share = (width + units) // copies
    return pl.pallas_call(
        ffn_grad_kernel,
        grid=(steps,),
        in_specs=[WIDE] * len(arrays),
        out_specs=pl.BlockSpec(
            (2, copies // (2 * steps), 2 * share, width), lambda m: (0, m, 0, 0)
        ),
        out_shape=pltpu.HBM((2, copies // 2, 2 * share, width), BF16),
        compiler_params=pltpu.CompilerParams(vmem_limit_bytes=ROOM),
        cost_estimate=cost(6),
        name="ffn_grad",
    )(*[near(array) for array in arrays])


def joint_grad_kernel(
    parts,
    normed_ref,
    query_ref,
    key_ref,
    value_ref,
    gain_ref,
    gain_two_ref,
    table_ref,
    branch_ref,
    mixed_ref,
    *refs,
):
    joint_grads = refs[:parts]
    out_ref, total, out_total = refs[parts:]
    row, at = turn()
    more = dot(
        jnp.concatenate([ref[row] for ref in joint_grads], axis=1), normed_ref[at(normed_ref)], 1, 0
    )
    more_out = dot(mixed_ref[at(mixed_ref)], branch_ref[at(branch_ref)], 1, 0)

    @pl.when(row == 0)
    def _():
        total[...] = more
        out_total[...] = more_out

    @pl.when(row > 0)
    def _():
        total[...] += more
        out_total[...] += more_out

    @pl.when(row == pl.num_programs(0) - 1)
    def _():
        width = out_ref.shape[2]
        wide = total.shape[0]
        inner = wide // 3
        cuts = out_ref.shape[0]
        gain_grad = (
            sum(
                jnp.sum(
                    total[part * inner : (part + 1) * inner] * ref[...].astype(F32),
                    axis=0,
                    keepdims=True,
                )
                for part, ref in enumerate((query_ref, key_ref, value_ref))
            )
            / gain_ref[...]
        )
        heads, _, size = table_ref.shape
        pad = jnp.zeros((1, width - size), F32)
        lines = [gain_grad, gain_two_ref[...]] + [
            jnp.concatenate([table_ref[head, 0:1], pad], axis=1) for head in range(heads)
        ]
        lines.append(jnp.zeros((8 - len(lines), width), F32))
        share, out_share = wide // cuts, inner // cuts
        for cut in range(cuts):
            out_ref[cut, 0:share] = total[cut * share : (cut + 1) * share].astype(BF16)
            low = share
            for a in range(parts):
                from_ = a * inner + cut * out_share
                out_ref[cut, low : low + out_share] = out_total[
                    from_ : from_ + out_share
                ].astype(BF16)
                low += out_share
            if cut == 0:
                out_ref[cut, low : low + 8] = jnp.concatenate(lines, axis=0).astype(BF16)
            else:
                out_ref[cut, low : low + 8] = jnp.zeros((8, width), BF16)


def joint_grad(
    normed, weights, gain, gain_two_grad, table_grad, grad_branch, joint_grads, mixed, copies
):
    rows, _, width = normed.shape
    wide = joint_grads[0].shape[1]
    inner = wide // 3
    parts = len(joint_grads)
    cuts = copies if inner % (8 * copies) == 0 else 1
    length = (wide + parts * inner) // cuts + 8
    return call(
        functools.partial(joint_grad_kernel, parts),
        "joint_grad",
        6,
        rows,
        [],
        [
            normed,
            *weights,
            gain,
            (gain_two_grad, "w"),
            (table_grad, "w"),
            (grad_branch, "h"),
            mixed,
            *joint_grads,
        ],
        [((cuts, length, width), BF16, "w")],
        [pltpu.VMEM((wide, width), F32), pltpu.VMEM((parts * inner, width), F32)],
    )[0]


def recut(values, wide, parts, inner, copies):
    width = values.shape[2]
    whole = values[0]
    out = [whole[:wide].reshape(copies, -1, width)]
    for a in range(parts):
        low = wide + a * inner
        out.append(whole[low : low + inner].reshape(copies, -1, width))
    extra = whole[None, wide + parts * inner :]
    out.append(jnp.concatenate([extra] + [jnp.zeros_like(extra)] * (copies - 1), axis=0))
    return jnp.concatenate(out, axis=1)


def hidden_grad_kernel(place_ref, weight_ref, middle_ref, hidden_ref, gain_ref, *refs):
    joint_grads, out_ref = refs[:-1], refs[-1]
    me = place_ref[0]
    row, at = turn()
    back = sum(dot(ref[row], weight_ref[a], 0, 0) for a, ref in enumerate(joint_grads))
    hidden = hidden_ref[at(hidden_ref)].astype(F32)
    scale = lax.rsqrt(jnp.mean(hidden * hidden, axis=-1, keepdims=True) + EPS)
    scaled = back * gain_ref[...]
    inner = jnp.mean(scaled * hidden, axis=-1, keepdims=True)
    out_ref[at(out_ref)] = (
        middle_ref[at(middle_ref)] + scale * scaled - hidden * (scale * scale * scale * inner)
    )


def hidden_grad(place, gathered, grad_middle, hidden, gain, joint_grads):
    return call(
        hidden_grad_kernel,
        "hidden_grad",
        150,
        hidden.shape[0],
        [place],
        [gathered, (grad_middle, "h"), (hidden, "h"), gain, *joint_grads],
        [(hidden.shape, F32, "h")],
    )[0]


def after(values, *others):
    return lax.optimization_barrier((values, *others))[0]


def swap(values, distance):
    parts = lax.axis_size("tp")
    return lax.ppermute(values, "tp", [(i, i ^ distance) for i in range(parts)])


def swap_all(blocks):
    return [blocks[0]] + [swap(block, a) for a, block in enumerate(blocks) if a]


def gather_line(values, first, second):
    pair = swap(values, 1)
    inner = [(1, 2), (2, 1)]
    outer = [(1, 0), (2, 3)]
    last_low = lax.ppermute(values, "tp", inner)
    pair, last_low, *first = lax.optimization_barrier((pair, last_low, *first))
    far_low = lax.ppermute(pair, "tp", inner)
    far_high = lax.ppermute(last_low, "tp", outer)
    far_low, far_high, *second = lax.optimization_barrier((far_low, far_high, *second))
    last_high = lax.ppermute(far_low, "tp", outer)
    return [values, pair, far_low, far_high, last_low, last_high], first, second


def across(values, bit):
    count = lax.axis_size("dp")
    return lax.ppermute(values, "dp", [(i, i ^ (1 << bit)) for i in range(count)])


def dp_bits():
    return range(lax.axis_size("dp").bit_length() - 1)


def join(values, other=None):
    place = lax.axis_index("dp")
    for bit in reversed(dp_bits()):
        upper = (place >> bit) & 1
        if bit == 0 and other is not None:
            values, other = lax.optimization_barrier((values, other))
        came = across(values, bit)
        values = jnp.where(
            upper == 1,
            jnp.concatenate((came, values), axis=0),
            jnp.concatenate((values, came), axis=0),
        )
    return values, other


def by_place(values):
    count = len(dp_bits())
    order = tuple(reversed(range(count))) + tuple(range(count, count + values.ndim - 1))
    return values.reshape((2,) * count + values.shape[1:]).transpose(order).reshape(values.shape)


def local(
    hidden_in,
    lengths,
    inst_lengths,
    w_query,
    w_key,
    w_value,
    attention_output_weight,
    feedforward_input_weight,
    feedforward_output_weight,
    rel_table,
    gain_attn,
    gain_ffn,
    grad_output,
    grad_pooled,
):
    rows, size, width = hidden_in.shape
    parts = lax.axis_size("tp")
    copies = lax.axis_size("dp")
    me = lax.axis_index("tp")
    group = lax.axis_index("dp")
    heads = rel_table.shape[1]
    inner = w_query.shape[1]
    tokens = rows * size
    place = me.astype(jnp.int32).reshape(1)
    gain_one = gain_attn.astype(F32).reshape(1, width)
    gain_two = gain_ffn.astype(F32).reshape(1, width)

    def share_of(weights):
        share = weights.shape[0] // copies
        return lax.dynamic_slice_in_dim(weights, group * share, share, 0)

    def fetched(shares, lead):
        everything = lax.all_gather(shares, "dp", axis=0, tiled=False)
        rest = everything[:, lead:].reshape(copies, parts, -1, width)
        return (
            jnp.swapaxes(rest, 0, 1).reshape(-1, width),
            everything[:, :lead].reshape(-1, width),
            everything,
        )

    first = norm_one(hidden_in, gain_one)
    attention_weights = jnp.concatenate(
        (w_query.T, w_key.T, w_value.T), axis=0
    )
    bias = bias_blocks(rel_table.T.astype(F32), parts, size)

    other_share = share_of(
        jnp.concatenate((feedforward_input_weight, feedforward_output_weight), axis=0)
    )
    ffn_share = other_share.shape[0]
    out_part = share_of(attention_output_weight)
    columns = grad_pooled.shape[1]
    spread = lax.dynamic_update_slice(
        jnp.zeros((rows, width), BF16), grad_pooled, (0, me * columns)
    )
    spread = swap_all([spread] * parts)
    blocks, (bias,), (out_part, other_share, *spread) = gather_line(
        first, [bias], [out_part, other_share] + spread
    )
    pool_cot = sum(block.astype(F32) for block in spread)
    counts = (lengths - inst_lengths).astype(F32)
    spots = me * size + jnp.arange(size, dtype=jnp.int32)
    mask = (
        (spots[None, :] >= inst_lengths[:, None]) & (spots[None, :] < lengths[:, None])
    ).astype(F32)
    grad_result = (
        grad_output.astype(F32)
        + pool_cot[:, None, :] * (mask / counts[:, None])[:, :, None]
    )
    grad_low = grad_result.astype(BF16).reshape(tokens, width)

    came = swap_all([out_part, out_part, jnp.concatenate((out_part, other_share), axis=0), out_part])
    out_size = out_part.shape[0]
    out_gathered, other_weights, _ = fetched(
        after(
            jnp.concatenate([came[2][out_size:]] + [block[:out_size] for block in came], axis=0),
            blocks[5],
        ),
        ffn_share,
    )
    blocks[5], grad_low = lax.optimization_barrier((blocks[5], grad_low))
    grad_low_pair = swap(grad_low, 1)
    came_joint = jnp.concatenate(
        swap_all([after(share_of(attention_weights), blocks[5])] * parts), axis=0
    )
    normed, joint, logs, *mixed = attend(
        place, lengths, blocks, (w_query.T, w_key.T, w_value.T), bias, heads
    )
    mixed, grad_low_pair, came_joint = lax.optimization_barrier((mixed, grad_low_pair, came_joint))
    gathered, _, joint_there = fetched(came_joint, 0)
    gathered = gathered.reshape(parts, -1, width)
    mixed = swap_all(mixed)
    middle, second, mixed = middle_of(out_gathered, hidden_in, gain_two, mixed)
    second = second.reshape(tokens, width)
    second_pair = swap(second, 1)

    weights = (feedforward_input_weight, feedforward_output_weight, other_weights)
    gelu, act, branch, back = feed_forward(second, grad_low, *weights)
    gelu_pair, act_pair, branch_pair, back_pair = feed_forward(
        second_pair, grad_low_pair, *weights
    )

    stacked = ffn_grad(
        (second, second_pair, grad_low, grad_low_pair, gelu, gelu_pair, act, act_pair), copies
    )
    summed = lax.psum_scatter(
        after(stacked, joint_there).reshape(-1, width), "dp", scatter_dimension=0, tiled=True
    )

    back_came = after(swap(back_pair, 1), stacked)

    grad_middle, grad_branch, gain_two_grad, *grad_mixed = middle_back(
        out_gathered,
        back.reshape(rows, size, width),
        back_came.reshape(rows, size, width),
        middle,
        grad_result,
        gain_two,
        parts,
    )
    grad_mixed = swap_all(grad_mixed)

    *joint_grads, table_grad = attend_back(place, lengths, joint, bias, logs, grad_mixed)
    came = swap_all(joint_grads)

    branch_came = swap(after(branch_pair, grad_mixed[-1]), 1)
    result = (
        middle
        + branch.reshape(rows, size, width).astype(F32)
        + branch_came.reshape(rows, size, width).astype(F32)
    )
    wide = 3 * inner
    heads_grad = joint_grad(
        normed,
        (w_query.T, w_key.T, w_value.T),
        gain_one,
        gain_two_grad,
        table_grad,
        grad_branch,
        joint_grads,
        mixed,
        copies,
    )
    if heads_grad.shape[0] != copies:
        heads_grad = recut(heads_grad, wide, parts, inner, copies)
    mine = lax.psum_scatter(
        heads_grad.reshape(-1, width), "dp", scatter_dimension=0, tiled=True
    )
    summed = after(summed, heads_grad)
    own_sum = summed[:ffn_share].astype(F32) + swap(summed[ffn_share:], 2).astype(F32)
    whole_ffn = lax.all_gather(own_sum.astype(BF16), "dp", axis=0, tiled=True).astype(F32)
    grad_hidden = hidden_grad(
        place,
        gathered,
        grad_middle,
        hidden_in,
        gain_one,
        [after(came[0], heads_grad, own_sum, branch_came)] + came[1:],
    )
    mine, result = after((mine, result), grad_hidden)

    layer_out = result.astype(BF16)
    pool_part = jnp.sum(result * mask[:, :, None], axis=1) / counts[:, None]
    pool_sum = pool_part + sum(swap(pool_part, a) for a in range(1, parts))
    pooled = lax.dynamic_slice_in_dim(pool_sum, me * columns, columns, 1)
    share, out_share = wide // copies, inner // copies
    extra = mine[share + parts * out_share :]
    moved = swap_all(
        [
            jnp.concatenate(
                (mine[share + a * out_share : share + (a + 1) * out_share], extra), axis=0
            )
            for a in range(parts)
        ]
    )
    moved = sum(block.astype(F32) for block in moved)
    whole, _ = join(
        jnp.concatenate(
            (
                mine[:share].astype(F32),
                moved[:out_share],
                moved[out_share : out_share + 2],
                extra[2:].astype(F32),
            ),
            axis=0,
        )[None].astype(BF16)
    )
    joint_sum = by_place(whole[:, :share]).reshape(wide, width).astype(F32)
    whole_out = by_place(whole[:, share : share + out_share]).reshape(inner, width).astype(F32)
    extra = whole[0, share + out_share :].astype(F32)
    table_sum = extra[2 : 2 + heads, : rel_table.shape[0]].T

    return (
        layer_out,
        pooled,
        grad_hidden,
        joint_sum[:inner].T,
        joint_sum[inner : 2 * inner].T,
        joint_sum[2 * inner : wide].T,
        whole_out,
        whole_ffn[:width],
        whole_ffn[width:],
        table_sum,
        extra[0],
        extra[1],
    )


def solution(mesh):
    in_specs = (
        P("dp", "tp", None),
        P("dp"),
        P("dp"),
        P(None, "tp"),
        P(None, "tp"),
        P(None, "tp"),
        P("tp", None),
        P(None, "tp"),
        P("tp", None),
        P(None, "tp"),
        P(),
        P(),
        P("dp", "tp", None),
        P("dp", "tp"),
    )
    out_specs = (
        P("dp", "tp", None),
        P("dp", "tp"),
        P("dp", "tp", None),
        P(None, "tp"),
        P(None, "tp"),
        P(None, "tp"),
        P("tp", None),
        P(None, "tp"),
        P("tp", None),
        P(None, "tp"),
        P(),
        P(),
    )
    return jax.shard_map(local, mesh=mesh, in_specs=in_specs, out_specs=out_specs, check_vma=False)
```

```python
import functools

import jax
import jax.numpy as jnp
from jax import lax
from jax.experimental import pallas as pl
from jax.experimental.pallas import tpu as pltpu
from jax.sharding import PartitionSpec as P

F32 = jnp.float32
BF16 = jnp.bfloat16
EPS = 1e-06
ROOM = 16 << 20
NEG = -1000000000.0
THRESHOLDS = (12, 16, 23, 32, 46, 64, 91)
GELU_C = 0.7978845608028654
GELU_K = 0.044715
WIDE = pl.BlockSpec(memory_space=pltpu.VMEM)
SCALARS = pl.BlockSpec(memory_space=pltpu.SMEM)


def dot(left, right, left_dim, right_dim, precision=None):
    return lax.dot_general(
        left,
        right,
        (((left_dim,), (right_dim,)), ((), ())),
        preferred_element_type=F32,
        precision=precision,
    )


def code_of(delta):
    n = abs(delta)
    far = 8 + sum(1 for threshold in THRESHOLDS if n >= threshold)
    return (16 if delta > 0 else 0) + (n if n < 8 else far)


def code_block(size, distance):
    shape = (size, size)
    delta = (
        lax.broadcasted_iota(jnp.int32, shape, 0)
        - lax.broadcasted_iota(jnp.int32, shape, 1)
        + size * distance
    )
    n = jnp.abs(delta)
    far = jnp.full(shape, 8, jnp.int32)
    for threshold in THRESHOLDS:
        far = far + (n >= threshold).astype(jnp.int32)
    return jnp.where(delta > 0, 16, 0) + jnp.where(n < 8, n, far)


def codes_in(size, distance):
    return sorted(
        {code_of(size * distance + inner) for inner in range(1 - size, size)}
    )


def cost(micros):
    return pl.CostEstimate(
        flops=int(micros * 1.1e9), bytes_accessed=int(micros * 1e6), transcendentals=0
    )


def shaped(shape, dtype):
    return jax.ShapeDtypeStruct(shape, dtype)


def near(values):
    return pltpu.with_memory_space_constraint(values, pltpu.VMEM)


def call(kernel, name, micros, rows, scalars, arrays, outs, scratch=()):
    def spec(shape, mark):
        if mark == "h":
            return pl.BlockSpec((1, *shape[1:]), lambda row: (row,) + (0,) * (len(shape) - 1))
        if mark == "w":
            return pl.BlockSpec(shape, lambda row: (0,) * len(shape))
        return WIDE

    marked = [(array if isinstance(array, tuple) else (array, "v")) for array in arrays]
    return pl.pallas_call(
        kernel,
        grid=(rows,),
        in_specs=[SCALARS] * len(scalars) + [spec(array.shape, mark) for array, mark in marked],
        out_specs=[spec(shape, mark) for shape, _, mark in outs],
        out_shape=[
            (pltpu.VMEM if mark == "v" else pltpu.HBM)(shape, dtype) for shape, dtype, mark in outs
        ],
        scratch_shapes=list(scratch),
        compiler_params=pltpu.CompilerParams(vmem_limit_bytes=ROOM),
        cost_estimate=cost(micros),
        name=name,
    )(
        *scalars,
        *[near(array) if mark == "v" else array for array, mark in marked],
    )


def turn():
    row = pl.program_id(0)
    return row, lambda ref: 0 if ref.shape[0] == 1 else row


def norm_kernel(x_ref, gain_ref, out_ref):
    gain = gain_ref[...]
    for row in range(x_ref.shape[0]):
        x = x_ref[row].astype(F32)
        scale = lax.rsqrt(jnp.mean(x * x, axis=-1, keepdims=True) + EPS)
        out_ref[row] = (x * scale * gain).astype(BF16)


def norm_one(hidden, gain):
    return call(norm_kernel, "norm_one", 2, 1, [], [hidden, gain], [(hidden.shape, BF16, "v")])[0]


def bias_kernel(parts, size, table_ref, out_ref):
    heads = out_ref.shape[0]
    for at in range(2 * parts - 1):
        distance = at - (parts - 1)
        present = codes_in(size, distance)
        codes = code_block(size, distance) if len(present) > 1 else None
        for head in range(heads):
            block = jnp.full((size, size), table_ref[head, present[0]], F32)
            for code in present[1:]:
                block = jnp.where(codes == code, table_ref[head, code], block)
            out_ref[head, at] = block


def bias_blocks(table, parts, size):
    heads = table.shape[0]
    return call(
        functools.partial(bias_kernel, parts, size),
        "bias_blocks",
        3,
        1,
        [table],
        [],
        [((heads, 2 * parts - 1, size, size), F32, "w")],
    )[0]


def chunk_bias(bias_ref, head, me, parts, first, count):
    return jnp.concatenate(
        [
            jnp.concatenate(
                [
                    bias_ref[head, (a_k ^ me) - (a_q ^ me) + parts - 1]
                    for a_q in range(first, first + count)
                ],
                axis=1,
            )
            for a_k in range(parts)
        ],
        axis=0,
    )


def chunk_valid(length, me, parts, size, count):
    inner = lax.broadcasted_iota(jnp.int32, (size, count * size), 0)
    return jnp.concatenate(
        [inner < length - (a_k ^ me) * size for a_k in range(parts)], axis=0
    )


def attend_kernel(
    heads,
    place_ref,
    length_ref,
    own_ref,
    pair_ref,
    far_low_ref,
    far_high_ref,
    last_low_ref,
    last_high_ref,
    query_ref,
    key_ref,
    value_ref,
    bias_ref,
    normed_ref,
    joint_ref,
    log_ref,
    *mixed_refs,
):
    parts = len(mixed_refs)
    size = own_ref.shape[1]
    me = place_ref[0]
    inner = joint_ref.shape[1] // 3
    head_size = inner // heads
    count = parts

    row, at = turn()
    out = at(normed_ref)
    normed_ref[out, 0:size] = own_ref[row]
    normed_ref[out, size : 2 * size] = pair_ref[row]
    normed_ref[out, 2 * size : 3 * size] = far_low_ref[row] + far_high_ref[row]
    normed_ref[out, 3 * size : 4 * size] = last_low_ref[row] + last_high_ref[row]
    for part, ref in enumerate((query_ref, key_ref, value_ref)):
        joint_ref[out, part * inner : (part + 1) * inner] = dot(
            ref[...], normed_ref[out], 1, 1
        ).astype(BF16)
    valid = chunk_valid(length_ref[row], me, parts, size, count)
    spans = [slice(head * head_size, (head + 1) * head_size) for head in range(heads)]
    scores = [
        dot(joint_ref[out, inner + span.start : inner + span.stop, :], joint_ref[out, span, :], 0, 0)
        for span in spans
    ]
    for head, span in enumerate(spans):
        biased = scores[head] + chunk_bias(bias_ref, head, me, parts, 0, parts)
        biased = jnp.where(valid, biased, NEG)
        peak = jnp.max(biased, axis=0, keepdims=True)
        raised = jnp.exp(biased - peak)
        total = jnp.sum(raised, axis=0, keepdims=True)
        scores[head] = (raised.astype(BF16), total)
        log_ref[out, head : head + 1, :] = peak + jnp.log(total)
    for head, span in enumerate(spans):
        raised, total = scores[head]
        value = joint_ref[out, 2 * inner + span.start : 2 * inner + span.stop, :]
        mixed = (dot(value, raised, 1, 0) / total).astype(BF16)
        for step in range(parts):
            mixed_refs[step][row, span, :] = mixed[:, step * size : (step + 1) * size]


def attend(place, lengths, blocks, weights, bias, heads):
    rows, size, width = blocks[0].shape
    parts = (bias.shape[1] + 1) // 2
    full = parts * size
    inner = weights[0].shape[0]
    return call(
        functools.partial(attend_kernel, heads),
        "attend",
        12,
        rows,
        [place, lengths],
        [*blocks, *weights, bias],
        [
            ((rows, full, width), BF16, "h"),
            ((rows, 3 * inner, full), BF16, "h"),
            ((rows, heads, full), F32, "h"),
        ]
        + [((rows, inner, size), BF16, "v")] * parts,
    )


def middle_kernel(weight_ref, hidden_ref, gain_ref, *refs):
    mixed_refs, (middle_ref, normed_ref, all_ref) = refs[:-3], refs[-3:]
    row, at = turn()
    mixed = jnp.concatenate([ref[row] for ref in mixed_refs], axis=0)
    all_ref[at(all_ref)] = mixed
    middle = hidden_ref[at(hidden_ref)].astype(F32) + dot(mixed, weight_ref[...], 0, 0)
    scale = lax.rsqrt(jnp.mean(middle * middle, axis=-1, keepdims=True) + EPS)
    middle_ref[at(middle_ref)] = middle
    normed_ref[row] = (middle * scale * gain_ref[...]).astype(BF16)


def middle_of(gathered, hidden, gain, mixed):
    rows, size, width = hidden.shape
    return call(
        middle_kernel,
        "middle_of",
        3,
        rows,
        [],
        [gathered, (hidden, "h"), gain, *mixed],
        [
            (hidden.shape, F32, "h"),
            (hidden.shape, BF16, "v"),
            ((rows, gathered.shape[0], size), BF16, "h"),
        ],
    )


def ffn_kernel(
    normed_ref,
    grad_ref,
    in_one_ref,
    in_two_ref,
    out_one_ref,
    out_two_ref,
    gelu_ref,
    act_ref,
    branch_ref,
    back_ref,
):
    shards = ((in_one_ref, out_one_ref), (in_two_ref, out_two_ref))
    for shard, (in_ref, out_ref) in enumerate(shards):
        v = dot(normed_ref[...], in_ref[...], 1, 0)
        grad_gelu = dot(grad_ref[...], out_ref[...], 1, 1).astype(BF16).astype(F32)
        square = v * v
        bent = jnp.tanh(GELU_C * (v + GELU_K * (square * v)))
        half = 0.5 * (1.0 + bent)
        slope = half + (0.5 * GELU_C) * v * (1.0 - bent * bent) * (
            1.0 + (3.0 * GELU_K) * square
        )
        gelu_ref[shard] = (v * half).astype(BF16)
        act_ref[shard] = (grad_gelu * slope).astype(BF16)
    back_ref[...] = sum(
        dot(act_ref[shard], in_ref[...], 1, 1) for shard, (in_ref, _) in enumerate(shards)
    ).astype(back_ref.dtype)
    branch_ref[...] = sum(
        dot(gelu_ref[shard], out_ref[...], 1, 0) for shard, (_, out_ref) in enumerate(shards)
    ).astype(branch_ref.dtype)


def feed_forward(normed, grad, w_in, w_out, other):
    tokens, width = normed.shape
    units = w_in.shape[1]
    return call(
        ffn_kernel,
        "feed_forward",
        6,
        1,
        [],
        [normed, grad, w_in, other[:width], w_out, other[width:]],
        [((2, tokens, units), BF16, "v")] * 2 + [((tokens, width), BF16, "w")] * 2,
    )


def middle_back_kernel(
    weight_ref,
    own_ref,
    other_ref,
    middle_ref,
    result_ref,
    gain_ref,
    grad_ref,
    low_ref,
    gain_grad_ref,
    *mixed_refs,
):
    row, at = turn()
    inner_size = mixed_refs[0].shape[1]
    back = own_ref[at(own_ref)].astype(F32) + other_ref[at(other_ref)].astype(F32)
    middle = middle_ref[at(middle_ref)]
    scale = lax.rsqrt(jnp.mean(middle * middle, axis=-1, keepdims=True) + EPS)
    scaled = back * gain_ref[...]
    inner = jnp.mean(scaled * middle, axis=-1, keepdims=True)
    grad = result_ref[at(result_ref)] + scale * scaled - middle * (scale * scale * scale * inner)
    gain_grad = jnp.sum(back * (middle * scale), axis=0, keepdims=True)

    @pl.when(row == 0)
    def _():
        gain_grad_ref[...] = gain_grad

    @pl.when(row > 0)
    def _():
        gain_grad_ref[...] += gain_grad

    grad_ref[at(grad_ref)] = grad
    low = grad.astype(BF16)
    low_ref[at(low_ref)] = low
    mixed = dot(weight_ref[...], low, 1, 1).astype(BF16)
    for a, ref in enumerate(mixed_refs):
        ref[row] = mixed[a * inner_size : (a + 1) * inner_size]


def middle_back(gathered, own, other, middle, grad_result, gain, parts):
    rows, size, width = middle.shape
    inner = gathered.shape[0] // parts
    return call(
        middle_back_kernel,
        "middle_back",
        4,
        rows,
        [],
        [gathered, (own, "h"), (other, "h"), (middle, "h"), (grad_result, "h"), gain],
        [(middle.shape, F32, "h"), (middle.shape, BF16, "h"), ((1, width), F32, "w")]
        + [((rows, inner, size), BF16, "v")] * parts,
    )


def attend_back_kernel(heads, parts, place_ref, length_ref, joint_ref, bias_ref, log_ref, *refs):
    mixed_refs = refs[:parts]
    joint_grads = refs[parts : 2 * parts]
    table_ref, sums = refs[2 * parts :]
    size = mixed_refs[0].shape[2]
    me = place_ref[0]
    inner = joint_ref.shape[1] // 3
    head_size = inner // heads
    count = parts
    row, at = turn()
    come = at(joint_ref)

    @pl.when(row == 0)
    def _():
        sums[...] = jnp.zeros_like(sums)

    valid = chunk_valid(length_ref[row], me, parts, size, count)
    for head in range(heads):
        low = head * head_size
        key_rows = slice(inner + low, inner + low + head_size)
        value_rows = slice(2 * inner + low, 2 * inner + low + head_size)
        key = joint_ref[come, key_rows, :]
        value = joint_ref[come, value_rows, :]
        grad_key = grad_value = None
        for first in range(0, parts, count):
            lanes = slice(first * size, (first + count) * size)
            query = joint_ref[come, low : low + head_size, lanes]
            grad_mixed = jnp.concatenate(
                [
                    mixed_refs[first + step][row, low : low + head_size, :]
                    for step in range(count)
                ],
                axis=1,
            )
            scores = dot(key, query, 0, 0) + chunk_bias(bias_ref, head, me, parts, first, count)
            probs = jnp.where(
                valid, jnp.exp(scores - log_ref[come, head : head + 1, lanes]), 0.0
            )
            grad_probs = dot(value, grad_mixed, 0, 0)
            inner_sum = jnp.sum(probs * grad_probs, axis=0, keepdims=True)
            grad_scores = probs * (grad_probs - inner_sum)
            low_scores = grad_scores.astype(BF16)
            more_value = dot(grad_mixed, probs.astype(BF16), 1, 1)
            more_key = dot(query, low_scores, 1, 1)
            grad_value = more_value if grad_value is None else grad_value + more_value
            grad_key = more_key if grad_key is None else grad_key + more_key
            grad_query = dot(key, low_scores, 1, 0).astype(BF16)
            for step in range(count):
                joint_grads[first + step][row, low : low + head_size, :] = grad_query[
                    :, step * size : (step + 1) * size
                ]
            for step in range(count):
                for a_k in range(parts):
                    place = (a_k ^ me) - ((first + step) ^ me) + parts - 1
                    sums[head, place] += grad_scores[
                        a_k * size : (a_k + 1) * size, step * size : (step + 1) * size
                    ]
        grad_key = grad_key.astype(BF16)
        grad_value = grad_value.astype(BF16)
        for a in range(parts):
            lanes = slice(a * size, (a + 1) * size)
            joint_grads[a][row, key_rows, :] = grad_key[:, lanes]
            joint_grads[a][row, value_rows, :] = grad_value[:, lanes]

    pl.when(row == pl.num_programs(0) - 1)(
        functools.partial(table_sums, heads, parts, size, sums, table_ref)
    )


def table_sums(heads, parts, size, sums, table_ref):
    ones = jnp.ones((8, size), F32)
    for head in range(heads):
        lines = [jnp.zeros((1, size), F32)] * 32
        for at in range(2 * parts - 1):
            distance = at - (parts - 1)
            present = codes_in(size, distance)
            codes = code_block(size, distance) if len(present) > 1 else None
            block = sums[head, at]
            for code in present:
                chosen = block if codes is None else jnp.where(codes == code, block, 0.0)
                lines[code] = lines[code] + jnp.sum(chosen, axis=0, keepdims=True)
        lined = jnp.concatenate(lines + [jnp.zeros((size - 32, size), F32)], axis=0)
        table_ref[head] = dot(ones, lined, 1, 1, lax.Precision.HIGHEST)


def attend_back(place, lengths, joint, bias, logs, mixed):
    rows, wide, full = joint.shape
    parts = len(mixed)
    heads = bias.shape[0]
    inner, size = mixed[0].shape[1:]
    return call(
        functools.partial(attend_back_kernel, heads, parts),
        "attend_back",
        14,
        rows,
        [place, lengths],
        [(joint, "h"), bias, (logs, "h"), *mixed],
        [((rows, wide, size), BF16, "v")] * parts + [((heads, 8, size), F32, "w")],
        [pltpu.VMEM(bias.shape, F32)],
    )


def ffn_grad_kernel(
    normed_ref,
    normed_pair_ref,
    grad_ref,
    grad_pair_ref,
    gelu_ref,
    gelu_pair_ref,
    act_ref,
    act_pair_ref,
    out_ref,
):
    half = pl.program_id(0)
    cuts = out_ref.shape[1]
    share = out_ref.shape[2] // 2
    size = cuts * share
    lanes = pl.ds(pl.multiple_of(half * size, size), size)
    normed = jnp.concatenate((normed_ref[:, lanes], normed_pair_ref[:, lanes]), axis=0)
    grad = jnp.concatenate((grad_ref[...], grad_pair_ref[...]), axis=0)
    for shard in range(2):
        act = jnp.concatenate((act_ref[shard], act_pair_ref[shard]), axis=0)
        gelu = jnp.concatenate(
            (gelu_ref[shard, :, lanes], gelu_pair_ref[shard, :, lanes]), axis=0
        )
        for side, (left, right) in enumerate(((normed, act), (gelu, grad))):
            total = dot(left, right, 0, 0).astype(BF16)
            for cut in range(cuts):
                out_ref[side, cut, shard * share : (shard + 1) * share] = total[
                    cut * share : (cut + 1) * share
                ]


def ffn_grad(arrays, copies):
    width, units = arrays[0].shape[1], arrays[4].shape[2]
    steps = 2
    share = (width + units) // copies
    return pl.pallas_call(
        ffn_grad_kernel,
        grid=(steps,),
        in_specs=[WIDE] * len(arrays),
        out_specs=pl.BlockSpec(
            (2, copies // (2 * steps), 2 * share, width), lambda m: (0, m, 0, 0)
        ),
        out_shape=pltpu.HBM((2, copies // 2, 2 * share, width), BF16),
        compiler_params=pltpu.CompilerParams(vmem_limit_bytes=ROOM),
        cost_estimate=cost(6),
        name="ffn_grad",
    )(*[near(array) for array in arrays])


def joint_grad_kernel(
    parts,
    normed_ref,
    query_ref,
    key_ref,
    value_ref,
    gain_ref,
    gain_two_ref,
    table_ref,
    branch_ref,
    mixed_ref,
    *refs,
):
    joint_grads = refs[:parts]
    out_ref, total, out_total = refs[parts:]
    row, at = turn()
    more = dot(
        jnp.concatenate([ref[row] for ref in joint_grads], axis=1), normed_ref[at(normed_ref)], 1, 0
    )
    more_out = dot(mixed_ref[at(mixed_ref)], branch_ref[at(branch_ref)], 1, 0)

    @pl.when(row == 0)
    def _():
        total[...] = more
        out_total[...] = more_out

    @pl.when(row > 0)
    def _():
        total[...] += more
        out_total[...] += more_out

    @pl.when(row == pl.num_programs(0) - 1)
    def _():
        width = out_ref.shape[2]
        wide = total.shape[0]
        inner = wide // 3
        cuts = out_ref.shape[0]
        gain_grad = (
            sum(
                jnp.sum(
                    total[part * inner : (part + 1) * inner] * ref[...].astype(F32),
                    axis=0,
                    keepdims=True,
                )
                for part, ref in enumerate((query_ref, key_ref, value_ref))
            )
            / gain_ref[...]
        )
        heads, _, size = table_ref.shape
        pad = jnp.zeros((1, width - size), F32)
        lines = [gain_grad, gain_two_ref[...]] + [
            jnp.concatenate([table_ref[head, 0:1], pad], axis=1) for head in range(heads)
        ]
        lines.append(jnp.zeros((8 - len(lines), width), F32))
        share, out_share = wide // cuts, inner // cuts
        for cut in range(cuts):
            out_ref[cut, 0:share] = total[cut * share : (cut + 1) * share].astype(BF16)
            low = share
            for a in range(parts):
                from_ = a * inner + cut * out_share
                out_ref[cut, low : low + out_share] = out_total[
                    from_ : from_ + out_share
                ].astype(BF16)
                low += out_share
            if cut == 0:
                out_ref[cut, low : low + 8] = jnp.concatenate(lines, axis=0).astype(BF16)
            else:
                out_ref[cut, low : low + 8] = jnp.zeros((8, width), BF16)


def joint_grad(
    normed, weights, gain, gain_two_grad, table_grad, grad_branch, joint_grads, mixed, copies
):
    rows, _, width = normed.shape
    wide = joint_grads[0].shape[1]
    inner = wide // 3
    parts = len(joint_grads)
    cuts = copies if inner % (8 * copies) == 0 else 1
    length = (wide + parts * inner) // cuts + 8
    return call(
        functools.partial(joint_grad_kernel, parts),
        "joint_grad",
        6,
        rows,
        [],
        [
            normed,
            *weights,
            gain,
            (gain_two_grad, "w"),
            (table_grad, "w"),
            (grad_branch, "h"),
            mixed,
            *joint_grads,
        ],
        [((cuts, length, width), BF16, "w")],
        [pltpu.VMEM((wide, width), F32), pltpu.VMEM((parts * inner, width), F32)],
    )[0]


def recut(values, wide, parts, inner, copies):
    width = values.shape[2]
    whole = values[0]
    out = [whole[:wide].reshape(copies, -1, width)]
    for a in range(parts):
        low = wide + a * inner
        out.append(whole[low : low + inner].reshape(copies, -1, width))
    extra = whole[None, wide + parts * inner :]
    out.append(jnp.concatenate([extra] + [jnp.zeros_like(extra)] * (copies - 1), axis=0))
    return jnp.concatenate(out, axis=1)


def hidden_grad_kernel(place_ref, weight_ref, middle_ref, hidden_ref, gain_ref, *refs):
    joint_grads, out_ref = refs[:-1], refs[-1]
    me = place_ref[0]
    row, at = turn()
    back = sum(dot(ref[row], weight_ref[a], 0, 0) for a, ref in enumerate(joint_grads))
    hidden = hidden_ref[at(hidden_ref)].astype(F32)
    scale = lax.rsqrt(jnp.mean(hidden * hidden, axis=-1, keepdims=True) + EPS)
    scaled = back * gain_ref[...]
    inner = jnp.mean(scaled * hidden, axis=-1, keepdims=True)
    out_ref[at(out_ref)] = (
        middle_ref[at(middle_ref)] + scale * scaled - hidden * (scale * scale * scale * inner)
    )


def hidden_grad(place, gathered, grad_middle, hidden, gain, joint_grads):
    return call(
        hidden_grad_kernel,
        "hidden_grad",
        150,
        hidden.shape[0],
        [place],
        [gathered, (grad_middle, "h"), (hidden, "h"), gain, *joint_grads],
        [(hidden.shape, F32, "h")],
    )[0]


def after(values, *others):
    return lax.optimization_barrier((values, *others))[0]


def swap(values, distance):
    parts = lax.axis_size("tp")
    return lax.ppermute(values, "tp", [(i, i ^ distance) for i in range(parts)])


def swap_all(blocks):
    return [blocks[0]] + [swap(block, a) for a, block in enumerate(blocks) if a]


def gather_line(values, first, second):
    pair = swap(values, 1)
    inner = [(1, 2), (2, 1)]
    outer = [(1, 0), (2, 3)]
    last_low = lax.ppermute(values, "tp", inner)
    pair, last_low, *first = lax.optimization_barrier((pair, last_low, *first))
    far_low = lax.ppermute(pair, "tp", inner)
    far_high = lax.ppermute(last_low, "tp", outer)
    far_low, far_high, *second = lax.optimization_barrier((far_low, far_high, *second))
    last_high = lax.ppermute(far_low, "tp", outer)
    return [values, pair, far_low, far_high, last_low, last_high], first, second


def across(values, bit):
    count = lax.axis_size("dp")
    return lax.ppermute(values, "dp", [(i, i ^ (1 << bit)) for i in range(count)])


def dp_bits():
    return range(lax.axis_size("dp").bit_length() - 1)


def join(values, other=None):
    place = lax.axis_index("dp")
    for bit in reversed(dp_bits()):
        upper = (place >> bit) & 1
        if bit == 0 and other is not None:
            values, other = lax.optimization_barrier((values, other))
        came = across(values, bit)
        values = jnp.where(
            upper == 1,
            jnp.concatenate((came, values), axis=0),
            jnp.concatenate((values, came), axis=0),
        )
    return values, other


def by_place(values):
    count = len(dp_bits())
    order = tuple(reversed(range(count))) + tuple(range(count, count + values.ndim - 1))
    return values.reshape((2,) * count + values.shape[1:]).transpose(order).reshape(values.shape)


def local(
    hidden_in,
    lengths,
    inst_lengths,
    w_query,
    w_key,
    w_value,
    attention_output_weight,
    feedforward_input_weight,
    feedforward_output_weight,
    rel_table,
    gain_attn,
    gain_ffn,
    grad_output,
    grad_pooled,
):
    rows, size, width = hidden_in.shape
    parts = lax.axis_size("tp")
    copies = lax.axis_size("dp")
    me = lax.axis_index("tp")
    group = lax.axis_index("dp")
    heads = rel_table.shape[1]
    inner = w_query.shape[1]
    tokens = rows * size
    place = me.astype(jnp.int32).reshape(1)
    gain_one = gain_attn.astype(F32).reshape(1, width)
    gain_two = gain_ffn.astype(F32).reshape(1, width)

    def share_of(weights):
        share = weights.shape[0] // copies
        return lax.dynamic_slice_in_dim(weights, group * share, share, 0)

    def fetched(shares, lead):
        everything = lax.all_gather(shares, "dp", axis=0, tiled=False)
        rest = everything[:, lead:].reshape(copies, parts, -1, width)
        return (
            jnp.swapaxes(rest, 0, 1).reshape(-1, width),
            everything[:, :lead].reshape(-1, width),
            everything,
        )

    first = norm_one(hidden_in, gain_one)
    attention_weights = jnp.concatenate(
        (w_query.T, w_key.T, w_value.T), axis=0
    )
    bias = bias_blocks(rel_table.T.astype(F32), parts, size)

    other_share = share_of(
        jnp.concatenate((feedforward_input_weight, feedforward_output_weight), axis=0)
    )
    ffn_share = other_share.shape[0]
    out_part = share_of(attention_output_weight)
    columns = grad_pooled.shape[1]
    spread = lax.dynamic_update_slice(
        jnp.zeros((rows, width), BF16), grad_pooled, (0, me * columns)
    )
    spread = swap_all([spread] * parts)
    blocks, (bias, *spread), (out_part, other_share, out_one, out_three) = gather_line(
        first, [bias] + spread, [out_part, other_share, swap(out_part, 1), swap(out_part, 3)]
    )
    pool_cot = sum(block.astype(F32) for block in spread)
    counts = (lengths - inst_lengths).astype(F32)
    spots = me * size + jnp.arange(size, dtype=jnp.int32)
    mask = (
        (spots[None, :] >= inst_lengths[:, None]) & (spots[None, :] < lengths[:, None])
    ).astype(F32)
    grad_result = (
        grad_output.astype(F32)
        + pool_cot[:, None, :] * (mask / counts[:, None])[:, :, None]
    )
    grad_low = grad_result.astype(BF16).reshape(tokens, width)

    came = [out_part, out_one, swap(jnp.concatenate((out_part, other_share), axis=0), 2), out_three]
    out_size = out_part.shape[0]
    out_gathered, other_weights, _ = fetched(
        after(
            jnp.concatenate([came[2][out_size:]] + [block[:out_size] for block in came], axis=0),
            blocks[5],
        ),
        ffn_share,
    )
    blocks[5], grad_low = lax.optimization_barrier((blocks[5], grad_low))
    grad_low_pair = swap(grad_low, 1)
    came_joint = jnp.concatenate(
        swap_all([after(share_of(attention_weights), blocks[5])] * parts), axis=0
    )
    normed, joint, logs, *mixed = attend(
        place, lengths, blocks, (w_query.T, w_key.T, w_value.T), bias, heads
    )
    mixed, grad_low_pair, came_joint = lax.optimization_barrier((mixed, grad_low_pair, came_joint))
    gathered, _, joint_there = fetched(came_joint, 0)
    gathered = gathered.reshape(parts, -1, width)
    mixed = swap_all(mixed)
    middle, second, mixed = middle_of(out_gathered, hidden_in, gain_two, mixed)
    second = second.reshape(tokens, width)
    second_pair = swap(second, 1)

    weights = (feedforward_input_weight, feedforward_output_weight, other_weights)
    gelu, act, branch, back = feed_forward(second, grad_low, *weights)
    gelu_pair, act_pair, branch_pair, back_pair = feed_forward(
        second_pair, grad_low_pair, *weights
    )

    stacked = ffn_grad(
        (second, second_pair, grad_low, grad_low_pair, gelu, gelu_pair, act, act_pair), copies
    )
    summed = lax.psum_scatter(
        after(stacked, joint_there).reshape(-1, width), "dp", scatter_dimension=0, tiled=True
    )

    back_came = after(swap(back_pair, 1), stacked)

    grad_middle, grad_branch, gain_two_grad, *grad_mixed = middle_back(
        out_gathered,
        back.reshape(rows, size, width),
        back_came.reshape(rows, size, width),
        middle,
        grad_result,
        gain_two,
        parts,
    )
    grad_mixed = swap_all(grad_mixed)

    *joint_grads, table_grad = attend_back(place, lengths, joint, bias, logs, grad_mixed)
    came = swap_all(joint_grads)

    branch_came = swap(after(branch_pair, grad_mixed[-1]), 1)
    result = (
        middle
        + branch.reshape(rows, size, width).astype(F32)
        + branch_came.reshape(rows, size, width).astype(F32)
    )
    wide = 3 * inner
    heads_grad = joint_grad(
        normed,
        (w_query.T, w_key.T, w_value.T),
        gain_one,
        gain_two_grad,
        table_grad,
        grad_branch,
        joint_grads,
        mixed,
        copies,
    )
    if heads_grad.shape[0] != copies:
        heads_grad = recut(heads_grad, wide, parts, inner, copies)
    mine = lax.psum_scatter(
        heads_grad.reshape(-1, width), "dp", scatter_dimension=0, tiled=True
    )
    summed = after(summed, heads_grad)
    own_sum = summed[:ffn_share].astype(F32) + swap(summed[ffn_share:], 2).astype(F32)
    whole_ffn = lax.all_gather(own_sum.astype(BF16), "dp", axis=0, tiled=True).astype(F32)
    grad_hidden = hidden_grad(
        place,
        gathered,
        grad_middle,
        hidden_in,
        gain_one,
        [after(came[0], heads_grad, own_sum, branch_came)] + came[1:],
    )
    mine, result = after((mine, result), grad_hidden)

    layer_out = result.astype(BF16)
    pool_part = jnp.sum(result * mask[:, :, None], axis=1) / counts[:, None]
    pool_sum = pool_part + sum(swap(pool_part, a) for a in range(1, parts))
    pooled = lax.dynamic_slice_in_dim(pool_sum, me * columns, columns, 1)
    share, out_share = wide // copies, inner // copies
    extra = mine[share + parts * out_share :]
    moved = swap_all(
        [
            jnp.concatenate(
                (mine[share + a * out_share : share + (a + 1) * out_share], extra), axis=0
            )
            for a in range(parts)
        ]
    )
    moved = sum(block.astype(F32) for block in moved)
    whole, _ = join(
        jnp.concatenate(
            (
                mine[:share].astype(F32),
                moved[:out_share],
                moved[out_share : out_share + 2],
                extra[2:].astype(F32),
            ),
            axis=0,
        )[None].astype(BF16)
    )
    joint_sum = by_place(whole[:, :share]).reshape(wide, width).astype(F32)
    whole_out = by_place(whole[:, share : share + out_share]).reshape(inner, width).astype(F32)
    extra = whole[0, share + out_share :].astype(F32)
    table_sum = extra[2 : 2 + heads, : rel_table.shape[0]].T

    return (
        layer_out,
        pooled,
        grad_hidden,
        joint_sum[:inner].T,
        joint_sum[inner : 2 * inner].T,
        joint_sum[2 * inner : wide].T,
        whole_out,
        whole_ffn[:width],
        whole_ffn[width:],
        table_sum,
        extra[0],
        extra[1],
    )


def solution(mesh):
    in_specs = (
        P("dp", "tp", None),
        P("dp"),
        P("dp"),
        P(None, "tp"),
        P(None, "tp"),
        P(None, "tp"),
        P("tp", None),
        P(None, "tp"),
        P("tp", None),
        P(None, "tp"),
        P(),
        P(),
        P("dp", "tp", None),
        P("dp", "tp"),
    )
    out_specs = (
        P("dp", "tp", None),
        P("dp", "tp"),
        P("dp", "tp", None),
        P(None, "tp"),
        P(None, "tp"),
        P(None, "tp"),
        P("tp", None),
        P(None, "tp"),
        P("tp", None),
        P(None, "tp"),
        P(),
        P(),
    )
    return jax.shard_map(local, mesh=mesh, in_specs=in_specs, out_specs=out_specs, check_vma=False)
```
